256 devices in a mesh: dp: 32 (over z, y), tensor: 8 (over x, core).
Axes of the slice: x: 4, y: 4, z: 8, core: 2. Of those that a mesh axis runs over, the one named last changes fastest.
Arguments:
- attention: bfloat16 [16384, 4096], P('dp', 'tensor'), may hold values from -0.44921875 to 0.546875
- cotangent: bfloat16 [16384, 2048], P('dp', 'tensor'), may hold values from -0.5 to 1.5
- projection: bfloat16 [4096, 2048], P(None, 'tensor'), may hold values from -0.125 to 0.125
Outputs:
- input_grad: bfloat16 [16384, 4096], P('dp', 'tensor')
- combined: float32 [4096, 2048], P(None, 'tensor')
The draws below stay inside these ranges and needn't reach their ends.
All inputs are finite; a program needn't handle non-finite values.
Results may differ from the reference program's by a relative error of at most 0.0004.
Values may be sent and summed in bfloat16 or wider, within the bound.
A program may use at most 64 MiB of HBM per device.

```python
import jax
import jax.numpy as jnp
from jax import lax

D = 2048
QD = 4096
ROWS_DEV = 512
TOKENS = 16384
N_DP = 32


def steps_of(stream_key, extent, shards, least, high):
    def one(position, shards_of):
        draws = jax.random.uniform(jax.random.fold_in(jax.random.fold_in(stream_key, 6), position), (shards_of,), jnp.float32, least / len(shards), high / len(shards))
        return jnp.repeat(jnp.exp(draws), extent[position] // shards_of).reshape((-1,) + (1,) * (len(extent) - position - 1))

    gain = one(*shards[0])
    for cut in shards[1:]:
        gain = gain * one(*cut)
    return gain


def bell_draw(stream_key, extent, deviation, most, shards=(), kind=jnp.bfloat16):
    result = deviation * jax.random.normal(stream_key, extent, jnp.float32)
    if shards:
        result = result * steps_of(stream_key, extent, shards, -0.22, 0.18)
    return jnp.clip(result, -most, most).astype(kind)


def setup_inputs(seed: int = 0) -> dict:
    splits = jax.random.split(jax.random.key(seed), 4)
    return {
        "attention": jnp.clip(-0.44921875 + 0.99609375 * jax.random.uniform(splits[0], (TOKENS, QD), jnp.float32) ** steps_of(splits[0], (TOKENS, QD), ((0, 32), (1, 8)), -0.2, 0.2), -0.44921875, 0.546875).astype(jnp.bfloat16),
        "cotangent": jnp.clip(-0.5 + 2.0 * jax.random.uniform(splits[1], (TOKENS, D), jnp.float32) ** steps_of(splits[1], (TOKENS, D), ((0, 32), (1, 8)), -0.2, 0.2), -0.5, 1.5).astype(jnp.bfloat16),
        "projection": bell_draw(splits[2], (QD, D), D ** -0.5, 0.125, ((1, 8),)),
    }


epsilon = 1e-06

def pair_merge(lower_vec, upper_vec):
    lower_sq = jnp.sum(lower_vec * lower_vec) + epsilon
    upper_sq = jnp.sum(upper_vec * upper_vec) + epsilon
    cross = jnp.sum(lower_vec * upper_vec)
    return (1.0 - cross / (2.0 * lower_sq)) * lower_vec + (1.0 - cross / (2.0 * upper_sq)) * upper_vec

def replica_grad(attention, cotangent, replica):
    row_start = replica * ROWS_DEV
    acts_rows = attention[row_start:row_start + ROWS_DEV]
    cot_rows = cotangent[row_start:row_start + ROWS_DEV]
    return jnp.dot(acts_rows.T, cot_rows, preferred_element_type=jnp.float32)

def tree_merge(attention, cotangent, first_index, span_size):
    if span_size == 1:
        return replica_grad(attention, cotangent, first_index)
    half_span = span_size // 2
    lower_vec = tree_merge(attention, cotangent, first_index, half_span)
    upper_vec = tree_merge(attention, cotangent, first_index + half_span, half_span)
    return pair_merge(lower_vec, upper_vec)

def reference(attention, cotangent, projection):

    def input_block(cot_rows):
        return jnp.dot(cot_rows, projection.T, preferred_element_type=jnp.float32).astype(jnp.bfloat16)
    blocks = lax.map(input_block, cotangent.reshape(N_DP, ROWS_DEV, D))
    input_grad = blocks.reshape(N_DP * ROWS_DEV, QD)
    combined = tree_merge(attention, cotangent, 0, N_DP)
    return (input_grad, combined)
```

```python
import jax
import jax.numpy as jnp
from jax import lax
from jax.sharding import Mesh
from jax.sharding import PartitionSpec as P

EPS = 1e-06


def tree_weights(gram, n):
    g = [[gram[i, j] for j in range(n)] for i in range(n)]
    w = [jnp.float32(1.0)] * n
    span = 1
    while len(g) > 1:
        half = len(g) // 2
        c = []
        for i in range(half):
            aa, bb, s = g[2 * i][2 * i], g[2 * i + 1][2 * i + 1], g[2 * i][2 * i + 1]
            c.append(1.0 - s / (2.0 * (aa + EPS)))
            c.append(1.0 - s / (2.0 * (bb + EPS)))
        w = [w[k] * c[k // span] for k in range(n)]
        span *= 2
        g = [
            [
                sum(c[a] * c[b] * g[a][b] for a in (2 * i, 2 * i + 1) for b in (2 * j, 2 * j + 1))
                for j in range(half)
            ]
            for i in range(half)
        ]
    return w


def merged(parts, axes):
    n = parts.shape[0]
    flat = [parts[i] for i in range(n)]
    dots = jnp.stack([jnp.sum(flat[i] * flat[j]) for i in range(n) for j in range(i, n)])
    dots = lax.psum(dots, axes)
    idx = {}
    k = 0
    for i in range(n):
        for j in range(i, n):
            idx[i, j] = idx[j, i] = dots[k]
            k += 1
    w = tree_weights(idx, n)
    return sum(w[i] * flat[i] for i in range(n))


def on_device(attention, cotangent, projection):
    full = lax.all_gather(cotangent, "tensor", axis=1, tiled=True)
    rows = lax.all_to_all(projection, "tensor", split_axis=0, concat_axis=1, tiled=True)
    input_grad = lax.dot_general(
        full, rows, (((1,), (1,)), ((), ())), preferred_element_type=jnp.float32
    ).astype(jnp.bfloat16)
    grad = lax.dot_general(
        attention, full, (((0,), (0,)), ((), ())), preferred_element_type=jnp.float32
    )
    parts = lax.all_to_all(grad.reshape(4, 128, 2048), "dp_1", 0, 0, tiled=True)
    quarter = merged(parts, ("dp_1", "tensor"))
    parts = lax.all_to_all(quarter.reshape(8, 16, 2048), "dp_0", 0, 0, tiled=True)
    piece = merged(parts, ("dp_0", "dp_1", "tensor"))
    piece = piece.reshape(16, 8, 256).transpose(1, 0, 2)
    piece = lax.all_to_all(piece, "tensor", 0, 0, tiled=True)
    gathered = lax.all_gather(piece, ("dp_0", "dp_1"), axis=0)
    combined = gathered.reshape(8, 4, 8, 16, 256).transpose(2, 1, 0, 3, 4).reshape(4096, 256)
    return (input_grad, combined)


def solution(mesh):
    finer = Mesh(mesh.devices.reshape(8, 4, mesh.shape["tensor"]), ("dp_0", "dp_1", "tensor"))
    dp = ("dp_0", "dp_1")
    return jax.shard_map(
        on_device,
        mesh=finer,
        in_specs=(P(dp, "tensor"), P(dp, "tensor"), P(None, "tensor")),
        out_specs=(P(dp, "tensor"), P(None, "tensor")),
        check_vma=False,
    )
```

```python
import jax
import jax.numpy as jnp
from jax import lax
from jax.experimental import pallas as pl
from jax.experimental.pallas import tpu as pltpu
from jax.sharding import PartitionSpec as P

EPS = 1e-06
MESH = pl.DeviceIdType.MESH
NX, NC, NY, NZ = 4, 2, 4, 8
NT = NX * NC
F32 = jnp.float32
BF16 = jnp.bfloat16
CUT = 80


def pairs(n):
    return [(i, j) for i in range(n) for j in range(i, n)]


def tree_weights(rows, n):
    table = {}
    for k, (i, j) in enumerate(pairs(n)):
        table[i, j] = table[j, i] = rows[k]
    weights = [None] * n
    span, m = 1, n
    while m > 1:
        half = m // 2
        coef = []
        for i in range(half):
            aa = jnp.maximum(table[2 * i, 2 * i], 0.0)
            bb = jnp.maximum(table[2 * i + 1, 2 * i + 1], 0.0)
            s = table[2 * i, 2 * i + 1]
            coef.append(1.0 - s / (2.0 * (aa + EPS)))
            coef.append(1.0 - s / (2.0 * (bb + EPS)))
        for k in range(n):
            c = coef[k // span]
            weights[k] = c if weights[k] is None else weights[k] * c
        if half > 1:
            new = {}
            for i in range(half):
                for j in range(i, half):
                    if i == j:
                        a, b = 2 * i, 2 * i + 1
                        v = (
                            coef[a] * coef[a] * table[a, a]
                            + coef[b] * coef[b] * table[b, b]
                            + 2.0 * (coef[a] * coef[b] * table[a, b])
                        )
                    else:
                        v = coef[2 * i] * (
                            coef[2 * j] * table[2 * i, 2 * j]
                            + coef[2 * j + 1] * table[2 * i, 2 * j + 1]
                        ) + coef[2 * i + 1] * (
                            coef[2 * j] * table[2 * i + 1, 2 * j]
                            + coef[2 * j + 1] * table[2 * i + 1, 2 * j + 1]
                        )
                    new[i, j] = new[j, i] = v
            table = new
        span, m = span * 2, half
    return weights


def body(
    att,
    cot,
    proj,
    igrad,
    comb,
    s1,
    ab,
    cb,
    cf,
    pb,
    g,
    mz,
    rz,
    st1,
    sr1,
    sr2,
    st2,
    tr1,
    tr2,
    tr3,
    fin,
    loc,
    a1s,
    a1r,
    b1s,
    b1r,
    c1s,
    c1r,
    cys,
    cyr,
    cfs,
    cfr,
    pbs,
    pbr,
    g1s,
    g1r,
    g2s,
    g2r,
    zs,
    zr,
    h1s,
    h1r,
    h2s,
    h2r,
    h3s,
    h3r,
    f1zs,
    f1zr,
    f1ys,
    f1yr,
    f2ys,
    f2yr,
    f2zs,
    f2zr,
):
    dp = lax.axis_index("dp")
    t = lax.axis_index("tensor")
    z, y = lax.div(dp, NY), lax.rem(dp, NY)
    x, c = lax.div(t, NC), lax.rem(t, NC)
    turn = 1 - 2 * c
    sib = 1 - c

    def xi(d):
        return lax.rem(x + d + NX, NX)

    def yi(d):
        return lax.rem(y + d + NY, NY)

    def zi(d):
        return lax.rem(z + d + NZ, NZ)

    def dev(z_=None, y_=None, t_=None):
        z_ = z if z_ is None else z_
        y_ = y if y_ is None else y_
        t_ = t if t_ is None else t_
        return {"dp": z_ * NY + y_, "tensor": t_}

    def copy(src, dst, ss, rs, to):
        return pltpu.make_async_remote_copy(
            src_ref=src, dst_ref=dst, send_sem=ss, recv_sem=rs, device_id=to, device_id_type=MESH
        )

    sent = []

    def send(src, dst, ss, rs, to):
        d = copy(src, dst, ss, rs, to)
        d.start()
        sent.append(d)

    def arrived(ref, ss, rs):
        copy(ref, ref, ss, rs, dev()).wait_recv()

    barrier = pltpu.get_barrier_semaphore()
    for j in range(1, NT):
        pl.semaphore_signal(barrier, 1, device_id=dev(t_=lax.rem(t + j, NT)), device_id_type=MESH)
    for j in range(1, NY):
        pl.semaphore_signal(barrier, 1, device_id=dev(y_=yi(j)), device_id_type=MESH)
    for j in range(1, NZ):
        pl.semaphore_signal(barrier, 1, device_id=dev(z_=zi(j)), device_id_type=MESH)
    own = [
        pltpu.make_async_copy(att.at[t], s1.at[t], loc.at[0]),
        pltpu.make_async_copy(cot, cb.at[y], loc.at[1]),
        pltpu.make_async_copy(cot, cf.at[t], loc.at[2]),
        pltpu.make_async_copy(proj.at[t], pb.at[t], loc.at[3]),
    ]
    for d in own:
        d.start()
    pl.semaphore_wait(barrier, (NT - 1) + (NY - 1) + (NZ - 1))

    for j in (4, 5, 3, 2, 6, 1, 7):
        to = lax.rem(t + j, NT)
        send(att.at[to], s1.at[t], a1s.at[j], a1r.at[t], dev(t_=to))
    send(cot, cb.at[y], cys.at[0], cyr.at[y], dev(y_=yi(1)))
    send(cot, cb.at[y], cys.at[1], cyr.at[y], dev(y_=yi(-1)))
    own[0].wait()
    for j in range(1, NT):
        s = lax.rem(t + j, NT)
        arrived(s1.at[s], a1s.at[0], a1r.at[s])
    for j in (2, 1, 3):
        q = yi(j)
        send(s1.at[pl.ds(2 * q, 2)], ab.at[t, y], b1s.at[j], b1r.at[y], dev(y_=q))
    mine = pltpu.make_async_copy(s1.at[pl.ds(2 * y, 2)], ab.at[t, y], loc.at[4])
    mine.start()
    yb, yf = yi(-turn), yi(turn)
    arrived(cb.at[yb], cys.at[0], cyr.at[yb])
    send(cb.at[yb], cb.at[yb], cys.at[2], cyr.at[yb], dev(y_=yf))
    for j in range(1, NY):
        q = yi(j)
        arrived(ab.at[t, q], b1s.at[0], b1r.at[q])
    mine.wait()

    class RowGather:
        def __init__(self, buf, ss, rs, first):
            self.buf, self.ss, self.rs = buf, ss, rs
            self.put(first, t, 0, NC * xi(1) + c)
            self.put(first, t, 1, NC * xi(-1) + c)
            self.put(first, t, 2, NC * x + sib)

        def put(self, src, slot, k, to):
            send(src, self.buf.at[slot], self.ss.at[k], self.rs.at[slot], dev(t_=to))

        def got(self, slot):
            arrived(self.buf.at[slot], self.ss.at[0], self.rs.at[slot])

        def forward(self):
            xb, xf = NC * xi(-turn) + c, NC * xi(turn) + c
            self.got(xb)
            self.put(self.buf.at[xb], xb, 3, xf)
            self.put(self.buf.at[xb], xb, 4, NC * x + sib)
            self.got(xf)
            self.put(self.buf.at[xf], xf, 5, NC * x + sib)

        def last(self):
            x2 = NC * xi(2) + c
            self.got(x2)
            self.put(self.buf.at[x2], x2, 6, NC * x + sib)

        def finish(self):
            for j in range(NX):
                self.got(NC * xi(j) + sib)

    rows = RowGather(ab, c1s, c1r, ab.at[t])
    rows.forward()
    rows.last()
    own[1].wait()
    arrived(cb.at[yf], cys.at[0], cyr.at[yf])
    y2 = yi(2)
    arrived(cb.at[y2], cys.at[0], cyr.at[y2])
    rows.finish()

    def grad(i, _):
        r, h = lax.div(i, 2), lax.rem(i, 2)
        a = ab[:, r, h].reshape(512, 512)
        v = lax.dot_general(cb[r], a, (((0,), (0,)), ((), ())), preferred_element_type=F32)
        for k in range(4):
            g[r, 4 * h + k] = v[:, 128 * k : 128 * (k + 1)]
        return 0

    lax.fori_loop(0, 8, grad, 0)

    def dots(load, n, steps, out):
        pn = pairs(n)

        def one(i, acc):
            v = [load(k, i) for k in range(n)]
            return tuple(a + v[p] * v[q] for a, (p, q) in zip(acc, pn))

        acc = lax.fori_loop(
            0, steps, one, tuple(jnp.zeros((8, 128), F32) for _ in pn), unroll=2
        )
        for k, a in enumerate(acc):
            out[k : k + 1, :] = jnp.sum(a, axis=0, keepdims=True)

    def load_g(k, i):
        return g[k, lax.div(i, 32), pl.ds(pl.multiple_of(lax.rem(i, 32) * 8, 8), 8), :]

    st1[...] = jnp.zeros_like(st1)
    dots(load_g, NY, 256, st1)

    def share(buf, slot, ss, rs, count, index, where):
        for j in range(1, count):
            send(buf.at[slot], buf.at[slot], ss.at[j], rs.at[slot], where(index(j)))
        for j in range(1, count):
            k = index(j)
            arrived(buf.at[k], ss.at[0], rs.at[k])
        total = buf[0]
        for k in range(1, count):
            total = total + buf[k]
        return total

    def ti(j):
        return lax.rem(t + j, NT)

    def full_rows(total, n):
        lanes = jnp.broadcast_to(jnp.sum(total, axis=1, keepdims=True), total.shape)
        return [lanes[k : k + 1, :] for k in range(len(pairs(n)))]

    sr1[t] = st1[...]
    sr2[y] = share(sr1, t, g1s, g1r, NT, ti, lambda k: dev(t_=k))
    total = share(sr2, y, g2s, g2r, NY, yi, lambda k: dev(y_=k))
    w = tree_weights(full_rows(total, NY), NY)

    def merge_into(dst, load, ws):
        def one(i, _):
            at = pl.ds(pl.multiple_of(i * 8, 8), 8)
            v = load(0, at) * ws[0]
            for k in range(1, len(ws)):
                v = v + load(k, at) * ws[k]
            dst[at, :] = v
            return 0

        lax.fori_loop(0, 32, one, 0)

    for j in (4, 3, 5, 2, 6, 1, 7, 0):
        zz = zi(j)
        merge_into(
            rz.at[z] if j == 0 else mz.at[zz], lambda k, at, zz=zz: g[k, zz, at, :], w
        )
        if j:
            send(mz.at[zz], rz.at[z], zs.at[j], zr.at[z], dev(z_=zz))

    cots = RowGather(cf, cfs, cfr, cot)
    for j in (1, 2, 3):
        send(proj.at[ti(j)], pb.at[t], pbs.at[j], pbr.at[t], dev(t_=ti(j)))
    cots.forward()
    cots.last()

    for j in range(1, NZ):
        k = zi(j)
        arrived(rz.at[k], zs.at[0], zr.at[k])

    def load_r(k, i):
        return rz[k, pl.ds(pl.multiple_of(i * 8, 8), 8), :]

    st2[...] = jnp.zeros_like(st2)
    dots(load_r, NZ, 32, st2)
    tr1[t] = st2[...]
    tr2[y] = share(tr1, t, h1s, h1r, NT, ti, lambda k: dev(t_=k))
    tr3[z] = share(tr2, y, h2s, h2r, NY, yi, lambda k: dev(y_=k))
    total = share(tr3, z, h3s, h3r, NZ, zi, lambda k: dev(z_=k))
    w = tree_weights(full_rows(total, NZ), NZ)
    merge_into(mz.at[z], lambda k, at: rz[k, at, :], w)
    fin[y, z] = jnp.transpose(mz[z])

    upper, lower = pl.ds(0, CUT), pl.ds(CUT, 128 - CUT)

    def f1z(zz, k, to):
        r = fin.at[y, zz, upper]
        send(r, r, f1zs.at[k], f1zr.at[zz], dev(z_=to))

    def f1z_got(zz):
        arrived(fin.at[y, zz, upper], f1zs.at[0], f1zr.at[zz])

    def f1y(yy, zz, k, to):
        r = fin.at[yy, zz, upper]
        send(r, r, f1ys.at[k, zz], f1yr.at[yy, zz], dev(y_=to))

    def f1y_got(yy, zz):
        arrived(fin.at[yy, zz, upper], f1ys.at[0, 0], f1yr.at[yy, zz])

    def f1y_start(zz):
        f1y(y, zz, 0, yf)
        f1y(y, zz, 1, yb)

    def f1y_forward(zz):
        f1y_got(yb, zz)
        f1y(yb, zz, 2, yf)

    def f2y(yy, k, to):
        r = fin.at[yy, z, lower]
        send(r, r, f2ys.at[k], f2yr.at[yy], dev(y_=to))

    def f2y_got(yy):
        arrived(fin.at[yy, z, lower], f2ys.at[0], f2yr.at[yy])

    def f2z(zz, k, to):
        r = fin.at[:, zz, lower]
        send(r, r, f2zs.at[k], f2zr.at[zz], dev(z_=to))

    def f2z_got(zz):
        arrived(fin.at[:, zz, lower], f2zs.at[0], f2zr.at[zz])

    zf, zb = zi(turn), zi(-turn)
    f1z(z, 0, zf)
    f1z(z, 1, zb)
    f2y(y, 0, yf)
    f2y(y, 1, yb)
    f1y_start(z)
    f2y_got(yb)
    f2y(yb, 2, yf)
    f2y_got(yf)
    for j in (4, 5, 6, 7):
        send(proj.at[ti(j)], pb.at[t], pbs.at[j], pbr.at[t], dev(t_=ti(j)))
    f1z_got(zb)
    f1z(zb, 2, zf)
    f1z_got(zf)
    f1z(zf, 3, zb)
    f2y_got(y2)
    f2z(z, 0, zf)
    f2z(z, 1, zb)
    f1y_start(zb)
    f1y_start(zf)
    f1y_forward(z)
    zb2, zf2 = zi(-2 * turn), zi(2 * turn)
    f1z_got(zb2)
    f1z(zb2, 4, zf)
    f1z_got(zf2)
    f1z(zf2, 5, zb)
    f1y_start(zb2)
    f1y_start(zf2)
    f2z_got(zb)
    f2z(zb, 2, zf)
    f2z_got(zf)
    f2z(zf, 3, zb)
    f1y_forward(zb)
    f1y_forward(zf)
    zb3, zf3, z4 = zi(-3 * turn), zi(3 * turn), zi(4)
    f1z_got(zb3)
    f1z(zb3, 6, zf)
    f1z_got(zf3)
    f1y_start(zb3)
    f1y_start(zf3)
    f1y_forward(zb2)
    f1y_forward(zf2)
    f2z_got(zb2)
    f2z(zb2, 4, zf)
    f2z_got(zf2)
    f2z(zf2, 5, zb)
    f1z_got(z4)
    f1y_start(z4)
    f1y_forward(zb3)
    f1y_forward(zf3)
    f2z_got(zb3)
    f2z(zb3, 6, zf)
    f1y_forward(z4)

    own[2].wait()
    own[3].wait()
    cots.finish()
    for j in range(1, NT):
        k = ti(j)
        arrived(pb.at[k], pbs.at[0], pbr.at[k])

    def part(i, _):
        at = pl.ds(pl.multiple_of(i * 128, 128), 128)
        v = jnp.zeros((128, 512), F32)
        for k in range(NT):
            v = v + lax.dot_general(
                cf[k, at, :], pb[k], (((1,), (1,)), ((), ())), preferred_element_type=F32
            )
        igrad[at, :] = v.astype(BF16)
        return 0

    lax.fori_loop(0, 4, part, 0)

    f2z_got(zf3)
    f2z_got(z4)
    for j in range(NZ):
        zz = zi(j)
        f1y_got(yf, zz)
        f1y_got(y2, zz)
    out = pltpu.make_async_copy(fin, comb, loc.at[5])
    out.start()
    for d in sent:
        d.wait_send()
    out.wait()


def on_device(attention, cotangent, projection):
    dma = pltpu.SemaphoreType.DMA
    v = pltpu.VMEM
    igrad, comb = pl.pallas_call(
        body,
        out_shape=(
            jax.ShapeDtypeStruct((512, 512), BF16),
            jax.ShapeDtypeStruct((NY, NZ, 128, 256), F32),
        ),
        in_specs=[pl.BlockSpec(memory_space=pl.ANY)] * 3,
        out_specs=(
            pl.BlockSpec(memory_space=pltpu.VMEM),
            pl.BlockSpec(memory_space=pl.ANY),
        ),
        scratch_shapes=[
            v((NT, 64, 512), BF16),
            v((NT, NY, 2, 64, 512), BF16),
            v((NY, 512, 256), BF16),
            v((NT, 512, 256), BF16),
            v((NT, 512, 256), BF16),
            v((NY, NZ, 256, 128), F32),
            v((NZ, 256, 128), F32),
            v((NZ, 256, 128), F32),
            v((16, 128), F32),
            v((NT, 16, 128), F32),
            v((NY, 16, 128), F32),
            v((40, 128), F32),
            v((NT, 40, 128), F32),
            v((NY, 40, 128), F32),
            v((NZ, 40, 128), F32),
            v((NY, NZ, 128, 256), F32),
            dma((6,)),
            dma((NT,)),
            dma((NT,)),
            dma((NY,)),
            dma((NY,)),
            dma((7,)),
            dma((NT,)),
            dma((3,)),
            dma((NY,)),
            dma((7,)),
            dma((NT,)),
            dma((NT,)),
            dma((NT,)),
            dma((NT,)),
            dma((NT,)),
            dma((NY,)),
            dma((NY,)),
            dma((NZ,)),
            dma((NZ,)),
            dma((NT,)),
            dma((NT,)),
            dma((NY,)),
            dma((NY,)),
            dma((NZ,)),
            dma((NZ,)),
            dma((7,)),
            dma((NZ,)),
            dma((3, NZ)),
            dma((NY, NZ)),
            dma((3,)),
            dma((NY,)),
            dma((7,)),
            dma((NZ,)),
        ],
        compiler_params=pltpu.CompilerParams(
            collective_id=0, has_side_effects=True, vmem_limit_bytes=48 * 1024 * 1024
        ),
        cost_estimate=pl.CostEstimate(
            flops=4 * 2**30, bytes_accessed=16 * 2**20, transcendentals=0
        ),
    )(
        attention.reshape(NT, 64, 512),
        cotangent,
        projection.reshape(NT, 512, 256),
    )
    return (igrad, comb.reshape(4096, 256))


def solution(mesh):
    return jax.shard_map(
        on_device,
        mesh=mesh,
        in_specs=(P("dp", "tensor"), P("dp", "tensor"), P(None, "tensor")),
        out_specs=(P("dp", "tensor"), P(None, "tensor")),
        check_vma=False,
    )
```

```python
import jax
import jax.numpy as jnp
from jax import lax
from jax.experimental import pallas as pl
from jax.experimental.pallas import tpu as pltpu
from jax.sharding import PartitionSpec as P

EPS = 1e-06
MESH = pl.DeviceIdType.MESH
NX, NC, NY, NZ = 4, 2, 4, 8
NT = NX * NC
F32 = jnp.float32
BF16 = jnp.bfloat16
CUT = 80


def pairs(n):
    return [(i, j) for i in range(n) for j in range(i, n)]


def tree_weights(rows, n):
    table = {}
    for k, (i, j) in enumerate(pairs(n)):
        table[i, j] = table[j, i] = rows[k]
    weights = [None] * n
    span, m = 1, n
    while m > 1:
        half = m // 2
        coef = []
        for i in range(half):
            aa = jnp.maximum(table[2 * i, 2 * i], 0.0)
            bb = jnp.maximum(table[2 * i + 1, 2 * i + 1], 0.0)
            s = table[2 * i, 2 * i + 1]
            coef.append(1.0 - s / (2.0 * (aa + EPS)))
            coef.append(1.0 - s / (2.0 * (bb + EPS)))
        for k in range(n):
            c = coef[k // span]
            weights[k] = c if weights[k] is None else weights[k] * c
        if half > 1:
            new = {}
            for i in range(half):
                for j in range(i, half):
                    if i == j:
                        a, b = 2 * i, 2 * i + 1
                        v = (
                            coef[a] * coef[a] * table[a, a]
                            + coef[b] * coef[b] * table[b, b]
                            + 2.0 * (coef[a] * coef[b] * table[a, b])
                        )
                    else:
                        v = coef[2 * i] * (
                            coef[2 * j] * table[2 * i, 2 * j]
                            + coef[2 * j + 1] * table[2 * i, 2 * j + 1]
                        ) + coef[2 * i + 1] * (
                            coef[2 * j] * table[2 * i + 1, 2 * j]
                            + coef[2 * j + 1] * table[2 * i + 1, 2 * j + 1]
                        )
                    new[i, j] = new[j, i] = v
            table = new
        span, m = span * 2, half
    return weights


def body(
    att,
    cot,
    proj,
    igrad,
    fin,
    s1,
    ab,
    cb,
    cf,
    pb,
    g,
    mz,
    rz,
    st1,
    sr1,
    sr2,
    st2,
    tr1,
    tr2,
    tr3,
    loc,
    a1s,
    a1r,
    b1s,
    b1r,
    c1s,
    c1r,
    cys,
    cyr,
    cfs,
    cfr,
    pxs,
    pxr,
    pzs,
    pzr,
    g1s,
    g1r,
    g2s,
    g2r,
    zs,
    zr,
    h1s,
    h1r,
    h2s,
    h2r,
    h3s,
    h3r,
    f1zs,
    f1zr,
    f1ys,
    f1yr,
    f2ys,
    f2yr,
    f2zs,
    f2zr,
):
    dp = lax.axis_index("dp")
    t = lax.axis_index("tensor")
    z, y = lax.div(dp, NY), lax.rem(dp, NY)
    x, c = lax.div(t, NC), lax.rem(t, NC)
    turn = 1 - 2 * c
    sib = 1 - c

    def xi(d):
        return lax.rem(x + d + NX, NX)

    def yi(d):
        return lax.rem(y + d + NY, NY)

    def zi(d):
        return lax.rem(z + d + NZ, NZ)

    def dev(z_=None, y_=None, t_=None):
        z_ = z if z_ is None else z_
        y_ = y if y_ is None else y_
        t_ = t if t_ is None else t_
        return {"dp": z_ * NY + y_, "tensor": t_}

    def copy(src, dst, ss, rs, to):
        return pltpu.make_async_remote_copy(
            src_ref=src, dst_ref=dst, send_sem=ss, recv_sem=rs, device_id=to, device_id_type=MESH
        )

    sent = []

    def send(src, dst, ss, rs, to):
        d = copy(src, dst, ss, rs, to)
        d.start()
        sent.append(d)

    def arrived(ref, ss, rs):
        copy(ref, ref, ss, rs, dev()).wait_recv()

    barrier = pltpu.get_barrier_semaphore()
    for j in range(1, NT):
        pl.semaphore_signal(barrier, 1, device_id=dev(t_=lax.rem(t + j, NT)), device_id_type=MESH)
    for j in range(1, NY):
        pl.semaphore_signal(barrier, 1, device_id=dev(y_=yi(j)), device_id_type=MESH)
    for j in range(1, NZ):
        pl.semaphore_signal(barrier, 1, device_id=dev(z_=zi(j)), device_id_type=MESH)
    own = [
        pltpu.make_async_copy(att.at[0, t], s1.at[0, t], loc.at[0]),
        pltpu.make_async_copy(att.at[1, t], s1.at[1, t], loc.at[1]),
        pltpu.make_async_copy(cot, cb.at[y], loc.at[2]),
        pltpu.make_async_copy(cot, cf.at[t], loc.at[3]),
        pltpu.make_async_copy(proj.at[t, z], pb.at[z, t], loc.at[4]),
    ]
    for d in own:
        d.start()
    pl.semaphore_wait(barrier, (NT - 1) + (NY - 1) + (NZ - 1))

    def ti(j):
        return lax.rem(t + j, NT)

    yb, yf, y2 = yi(-turn), yi(turn), yi(2)

    class RowGather:
        def __init__(self, buf, ss, rs, first):
            self.buf, self.ss, self.rs = buf, ss, rs
            self.put(first, t, 0, NC * xi(1) + c)
            self.put(first, t, 1, NC * xi(-1) + c)
            self.put(first, t, 2, NC * x + sib)

        def put(self, src, slot, k, to):
            send(src, self.buf.at[slot], self.ss.at[k], self.rs.at[slot], dev(t_=to))

        def got(self, slot):
            arrived(self.buf.at[slot], self.ss.at[0], self.rs.at[slot])

        def forward(self):
            xb, xf = NC * xi(-turn) + c, NC * xi(turn) + c
            self.got(xb)
            self.put(self.buf.at[xb], xb, 3, xf)
            self.put(self.buf.at[xb], xb, 4, NC * x + sib)
            self.got(xf)
            self.put(self.buf.at[xf], xf, 5, NC * x + sib)

        def last(self):
            x2 = NC * xi(2) + c
            self.got(x2)
            self.put(self.buf.at[x2], x2, 6, NC * x + sib)

        def finish(self):
            for j in range(NX):
                self.got(NC * xi(j) + sib)

    class DepthRing:
        def __init__(self, block, ss, rs):
            self.block, self.ss, self.rs = block, ss, rs
            self.put(z, 0, zi(turn))
            self.put(z, 1, zi(-turn))

        def put(self, zz, k, to):
            r = self.block(zz)
            send(r, r, self.ss.at[k], self.rs.at[zz], dev(z_=to))

        def got(self, zz):
            arrived(self.block(zz), self.ss.at[0], self.rs.at[zz])

        def far(self, h):
            zz = zi(-h * turn)
            self.got(zz)
            if h < 4:
                self.put(zz, 2 * h, zi(turn))
            return zz

        def near(self, h):
            zz = zi(h * turn)
            self.got(zz)
            if h < 3:
                self.put(zz, 2 * h + 1, zi(-turn))
            return zz

    for h in range(2):
        for j in (4, 5, 3, 2, 6, 1, 7):
            to = ti(j)
            send(att.at[h, to], s1.at[h, t], a1s.at[h, j], a1r.at[h, t], dev(t_=to))
    send(cot, cb.at[y], cys.at[0], cyr.at[y], dev(y_=yi(1)))
    send(cot, cb.at[y], cys.at[1], cyr.at[y], dev(y_=yi(-1)))
    for j in (4, 5, 3, 2, 6, 1, 7):
        to = ti(j)
        send(proj.at[to, z], pb.at[z, t], pxs.at[j], pxr.at[t], dev(t_=to))
    mine = []
    for h in range(2):
        own[h].wait()
        for j in range(1, NT):
            s = ti(j)
            arrived(s1.at[h, s], a1s.at[h, 0], a1r.at[h, s])
        for j in (2, 1, 3):
            q = yi(j)
            send(s1.at[h, pl.ds(2 * q, 2)], ab.at[h, t, y], b1s.at[h, j], b1r.at[h, y], dev(y_=q))
        mine.append(
            pltpu.make_async_copy(s1.at[h, pl.ds(2 * y, 2)], ab.at[h, t, y], loc.at[5 + h])
        )
        mine[h].start()

    def row_ready(h):
        for j in range(1, NY):
            q = yi(j)
            arrived(ab.at[h, t, q], b1s.at[h, 0], b1r.at[h, q])
        mine[h].wait()
        return RowGather(ab.at[h], c1s.at[h], c1r.at[h], ab.at[h, t])

    rows0 = row_ready(0)
    own[4].wait()
    for j in range(1, NT):
        k = ti(j)
        arrived(pb.at[z, k], pxs.at[0], pxr.at[k])
    depth = DepthRing(lambda zz: pb.at[zz], pzs, pzr)
    arrived(cb.at[yb], cys.at[0], cyr.at[yb])
    send(cb.at[yb], cb.at[yb], cys.at[2], cyr.at[yb], dev(y_=yf))
    rows1 = row_ready(1)
    rows0.forward()
    rows1.forward()
    own[2].wait()
    arrived(cb.at[yf], cys.at[0], cyr.at[yf])
    arrived(cb.at[y2], cys.at[0], cyr.at[y2])
    rows0.last()
    depth.far(1)
    depth.near(1)
    rows0.finish()

    def grad(h):
        def one(i, _):
            r, b = lax.div(i, 2), lax.rem(i, 2)
            a = ab[h, :, r, b].reshape(256, 512)
            v = lax.dot_general(
                cb[r, 256 * h : 256 * (h + 1), :],
                a,
                (((0,), (0,)), ((), ())),
                preferred_element_type=F32,
            )
            for k in range(4):
                u = v[:, 128 * k : 128 * (k + 1)]
                g[r, 4 * b + k] = u if h == 0 else g[r, 4 * b + k] + u
            return 0

        lax.fori_loop(0, 8, one, 0)

    grad(0)
    rows1.last()
    rows1.finish()
    grad(1)
    depth.far(2)
    depth.near(2)

    def dots(load, n, steps, out):
        pn = pairs(n)

        def one(i, acc):
            v = [load(k, i) for k in range(n)]
            return tuple(a + v[p] * v[q] for a, (p, q) in zip(acc, pn))

        acc = lax.fori_loop(
            0, steps, one, tuple(jnp.zeros((8, 128), F32) for _ in pn), unroll=2
        )
        for k, a in enumerate(acc):
            out[k : k + 1, :] = jnp.sum(a, axis=0, keepdims=True)

    def load_g(k, i):
        return g[k, lax.div(i, 32), pl.ds(pl.multiple_of(lax.rem(i, 32) * 8, 8), 8), :]

    st1[...] = jnp.zeros_like(st1)
    dots(load_g, NY, 256, st1)

    def share(buf, slot, ss, rs, count, index, where):
        for j in range(1, count):
            send(buf.at[slot], buf.at[slot], ss.at[j], rs.at[slot], where(index(j)))
        for j in range(1, count):
            k = index(j)
            arrived(buf.at[k], ss.at[0], rs.at[k])
        total = buf[0]
        for k in range(1, count):
            total = total + buf[k]
        return total

    def full_rows(total, n):
        lanes = jnp.broadcast_to(jnp.sum(total, axis=1, keepdims=True), total.shape)
        return [lanes[k : k + 1, :] for k in range(len(pairs(n)))]

    sr1[t] = st1[...]
    sr2[y] = share(sr1, t, g1s, g1r, NT, ti, lambda k: dev(t_=k))
    cots = RowGather(cf, cfs, cfr, cot)
    total = share(sr2, y, g2s, g2r, NY, yi, lambda k: dev(y_=k))
    depth.far(3)
    w = tree_weights(full_rows(total, NY), NY)

    def merge_into(dst, load, ws):
        def one(i, _):
            at = pl.ds(pl.multiple_of(i * 8, 8), 8)
            v = load(0, at) * ws[0]
            for k in range(1, len(ws)):
                v = v + load(k, at) * ws[k]
            dst[at, :] = v
            return 0

        lax.fori_loop(0, 32, one, 0)

    for j in (4, 3, 5, 2, 6, 1, 7, 0):
        zz = zi(j)
        merge_into(
            rz.at[z] if j == 0 else mz.at[zz], lambda k, at, zz=zz: g[k, zz, at, :], w
        )
        if j:
            send(mz.at[zz], rz.at[z], zs.at[j], zr.at[z], dev(z_=zz))

    cots.forward()
    cots.last()
    depth.near(3)
    depth.far(4)
    own[3].wait()
    cots.finish()

    def part(i, _):
        k0, k1 = lax.div(i, 4), lax.rem(i, 4)
        at = pl.ds(pl.multiple_of(k0 * 256, 256), 256)
        v = jnp.zeros((256, 128), F32)
        for k in range(NT):
            b = pb[pl.ds(2 * k1, 2), k].reshape(128, 256)
            v = v + lax.dot_general(
                cf[k, at, :], b, (((1,), (1,)), ((), ())), preferred_element_type=F32
            )
        igrad[at, pl.ds(pl.multiple_of(k1 * 128, 128), 128)] = v.astype(BF16)
        return 0

    lax.fori_loop(0, 8, part, 0)

    for j in range(1, NZ):
        k = zi(j)
        arrived(rz.at[k], zs.at[0], zr.at[k])

    def load_r(k, i):
        return rz[k, pl.ds(pl.multiple_of(i * 8, 8), 8), :]

    st2[...] = jnp.zeros_like(st2)
    dots(load_r, NZ, 32, st2)
    tr1[t] = st2[...]
    tr2[y] = share(tr1, t, h1s, h1r, NT, ti, lambda k: dev(t_=k))
    tr3[z] = share(tr2, y, h2s, h2r, NY, yi, lambda k: dev(y_=k))
    total = share(tr3, z, h3s, h3r, NZ, zi, lambda k: dev(z_=k))
    w = tree_weights(full_rows(total, NZ), NZ)
    merge_into(mz.at[z], lambda k, at: rz[k, at, :], w)
    fin[y, z] = jnp.transpose(mz[z])

    upper, lower = pl.ds(0, CUT), pl.ds(CUT, 128 - CUT)

    def f1y(yy, zz, k, to):
        r = fin.at[yy, zz, upper]
        send(r, r, f1ys.at[k, zz], f1yr.at[yy, zz], dev(y_=to))

    def f1y_got(yy, zz):
        arrived(fin.at[yy, zz, upper], f1ys.at[0, 0], f1yr.at[yy, zz])

    def f1y_start(zz):
        f1y(y, zz, 0, yf)
        f1y(y, zz, 1, yb)

    def f1y_forward(zz):
        f1y_got(yb, zz)
        f1y(yb, zz, 2, yf)

    def f2y(yy, k, to):
        r = fin.at[yy, z, lower]
        send(r, r, f2ys.at[k], f2yr.at[yy], dev(y_=to))

    def f2y_got(yy):
        arrived(fin.at[yy, z, lower], f2ys.at[0], f2yr.at[yy])

    ring1 = DepthRing(lambda zz: fin.at[y, zz, upper], f1zs, f1zr)
    f2y(y, 0, yf)
    f2y(y, 1, yb)
    f1y_start(z)
    f2y_got(yb)
    f2y(yb, 2, yf)
    f2y_got(yf)
    f2y_got(y2)
    ring2 = DepthRing(lambda zz: fin.at[:, zz, lower], f2zs, f2zr)
    done = [z]
    for h in range(1, 5):
        new = [ring1.far(h)]
        if h < 4:
            new.append(ring1.near(h))
        for zz in new:
            f1y_start(zz)
        for zz in done:
            f1y_forward(zz)
        done = new
        ring2.far(h)
        if h < 4:
            ring2.near(h)
    for zz in done:
        f1y_forward(zz)
    for j in range(NZ):
        zz = zi(j)
        f1y_got(yf, zz)
        f1y_got(y2, zz)
    for d in sent:
        d.wait_send()


def on_device(attention, cotangent, projection):
    dma = pltpu.SemaphoreType.DMA

    def hbm(a):
        return pltpu.with_memory_space_constraint(a, pltpu.HBM)

    v = pltpu.VMEM
    igrad, comb = pl.pallas_call(
        body,
        out_shape=(
            jax.ShapeDtypeStruct((512, 512), BF16),
            jax.ShapeDtypeStruct((NY, NZ, 128, 256), F32),
        ),
        in_specs=[pl.BlockSpec(memory_space=pl.ANY)] * 3,
        out_specs=(
            pl.BlockSpec(memory_space=pltpu.VMEM),
            pl.BlockSpec(memory_space=pltpu.VMEM),
        ),
        scratch_shapes=[
            v((2, NT, 32, 512), BF16),
            v((2, NT, NY, 2, 32, 512), BF16),
            v((NY, 512, 256), BF16),
            v((NT, 512, 256), BF16),
            v((NZ, NT, 64, 256), BF16),
            v((NY, NZ, 256, 128), F32),
            v((NZ, 256, 128), F32),
            v((NZ, 256, 128), F32),
            v((16, 128), F32),
            v((NT, 16, 128), F32),
            v((NY, 16, 128), F32),
            v((40, 128), F32),
            v((NT, 40, 128), F32),
            v((NY, 40, 128), F32),
            v((NZ, 40, 128), F32),
            dma((7,)),
            dma((2, NT)),
            dma((2, NT)),
            dma((2, NY)),
            dma((2, NY)),
            dma((2, 7)),
            dma((2, NT)),
            dma((3,)),
            dma((NY,)),
            dma((7,)),
            dma((NT,)),
            dma((NT,)),
            dma((NT,)),
            dma((8,)),
            dma((NZ,)),
            dma((NT,)),
            dma((NT,)),
            dma((NY,)),
            dma((NY,)),
            dma((NZ,)),
            dma((NZ,)),
            dma((NT,)),
            dma((NT,)),
            dma((NY,)),
            dma((NY,)),
            dma((NZ,)),
            dma((NZ,)),
            dma((7,)),
            dma((NZ,)),
            dma((3, NZ)),
            dma((NY, NZ)),
            dma((3,)),
            dma((NY,)),
            dma((7,)),
            dma((NZ,)),
        ],
        compiler_params=pltpu.CompilerParams(
            collective_id=0, has_side_effects=True, vmem_limit_bytes=48 * 1024 * 1024
        ),
        cost_estimate=pl.CostEstimate(
            flops=4 * 2**30, bytes_accessed=16 * 2**20, transcendentals=0
        ),
    )(
        hbm(attention.reshape(2, NT, 32, 512)),
        hbm(cotangent),
        hbm(projection.reshape(NT, NZ, 64, 256)),
    )
    return (igrad, comb.reshape(4096, 256))


def solution(mesh):
    return jax.shard_map(
        on_device,
        mesh=mesh,
        in_specs=(P("dp", "tensor"), P("dp", "tensor"), P(None, "tensor")),
        out_specs=(P("dp", "tensor"), P(None, "tensor")),
        check_vma=False,
    )
```

```python
import math

import jax
import jax.numpy as jnp
from jax import lax
from jax.experimental import pallas as pl
from jax.experimental.pallas import tpu as pltpu
from jax.sharding import PartitionSpec as P

EPS = 1e-06
MESH = pl.DeviceIdType.MESH
NX, NC, NY, NZ = 4, 2, 4, 8
NT = NX * NC
F32 = jnp.float32
BF16 = jnp.bfloat16
CUT = 96


MU_Z = 2.0**10 - 1
MU_F = 2.0**18 - 1


def encode(v, inv, mu):
    k = jnp.log(1.0 + jnp.abs(v) * (inv * mu)) * (240.0 / math.log(1.0 + mu)) - 120.0
    e = jnp.exp2(k)
    return jnp.where(v < 0, -e, e).astype(BF16)


def decode(q, scale, mu):
    q = q.astype(F32)
    a = math.log(1.0 + mu) / 240.0
    h = jnp.log(jnp.abs(q)) * (a / math.log(2.0)) + 120.0 * a
    u = (jnp.exp(h) - 1.0) * (scale * (1.0 / mu))
    return jnp.where(q < 0, -u, u)


def pairs(n):
    return [(i, j) for i in range(n) for j in range(i, n)]


def tree_weights(rows, n):
    table = {}
    for k, (i, j) in enumerate(pairs(n)):
        table[i, j] = table[j, i] = rows[k]
    weights = [None] * n
    span, m = 1, n
    while m > 1:
        half = m // 2
        coef = []
        for i in range(half):
            aa = jnp.maximum(table[2 * i, 2 * i], 0.0)
            bb = jnp.maximum(table[2 * i + 1, 2 * i + 1], 0.0)
            s = table[2 * i, 2 * i + 1]
            coef.append(1.0 - s / (2.0 * (aa + EPS)))
            coef.append(1.0 - s / (2.0 * (bb + EPS)))
        for k in range(n):
            c = coef[k // span]
            weights[k] = c if weights[k] is None else weights[k] * c
        if half > 1:
            new = {}
            for i in range(half):
                for j in range(i, half):
                    if i == j:
                        a, b = 2 * i, 2 * i + 1
                        v = (
                            coef[a] * coef[a] * table[a, a]
                            + coef[b] * coef[b] * table[b, b]
                            + 2.0 * (coef[a] * coef[b] * table[a, b])
                        )
                    else:
                        v = coef[2 * i] * (
                            coef[2 * j] * table[2 * i, 2 * j]
                            + coef[2 * j + 1] * table[2 * i, 2 * j + 1]
                        ) + coef[2 * i + 1] * (
                            coef[2 * j] * table[2 * i + 1, 2 * j]
                            + coef[2 * j + 1] * table[2 * i + 1, 2 * j + 1]
                        )
                    new[i, j] = new[j, i] = v
            table = new
        span, m = span * 2, half
    return weights


def body(
    att,
    cot,
    proj,
    igrad,
    fin,
    s1,
    ab,
    cb,
    cf,
    pb,
    g,
    mz,
    rz,
    qz,
    rq,
    fc,
    mt,
    st,
    sr,
    tr1,
    tr2,
    loc,
    a1s,
    a1r,
    b1s,
    b1r,
    c1s,
    c1r,
    cys,
    cyr,
    cfs,
    cfr,
    pxs,
    pxr,
    pzs,
    pzr,
    g1s,
    g1r,
    zs,
    zr,
    h1s,
    h1r,
    h2s,
    h2r,
    f1zs,
    f1zr,
    f1ys,
    f1yr,
    f2ys,
    f2yr,
    f2zs,
    f2zr,
):
    dp = lax.axis_index("dp")
    t = lax.axis_index("tensor")
    z, y = lax.div(dp, NY), lax.rem(dp, NY)
    x, c = lax.div(t, NC), lax.rem(t, NC)
    turn = 1 - 2 * c
    sib = 1 - c

    def xi(d):
        return lax.rem(x + d + NX, NX)

    def yi(d):
        return lax.rem(y + d + NY, NY)

    def zi(d):
        return lax.rem(z + d + NZ, NZ)

    def dev(z_=None, y_=None, t_=None):
        z_ = z if z_ is None else z_
        y_ = y if y_ is None else y_
        t_ = t if t_ is None else t_
        return {"dp": z_ * NY + y_, "tensor": t_}

    def copy(src, dst, ss, rs, to):
        return pltpu.make_async_remote_copy(
            src_ref=src, dst_ref=dst, send_sem=ss, recv_sem=rs, device_id=to, device_id_type=MESH
        )

    sent = []

    def send(src, dst, ss, rs, to):
        d = copy(src, dst, ss, rs, to)
        d.start()
        sent.append(d)

    def arrived(ref, ss, rs):
        copy(ref, ref, ss, rs, dev()).wait_recv()

    barrier = pltpu.get_barrier_semaphore()
    for j in range(1, NT):
        pl.semaphore_signal(barrier, 1, device_id=dev(t_=lax.rem(t + j, NT)), device_id_type=MESH)
    for j in range(1, NY):
        pl.semaphore_signal(barrier, 1, device_id=dev(y_=yi(j)), device_id_type=MESH)
    for j in range(1, NZ):
        pl.semaphore_signal(barrier, 1, device_id=dev(z_=zi(j)), device_id_type=MESH)
    own = [
        pltpu.make_async_copy(att.at[0, t], s1.at[0, t], loc.at[0]),
        pltpu.make_async_copy(att.at[1, t], s1.at[1, t], loc.at[1]),
        pltpu.make_async_copy(cot, cb.at[y], loc.at[2]),
        pltpu.make_async_copy(cot, cf.at[t], loc.at[3]),
        pltpu.make_async_copy(proj.at[t, z], pb.at[z, t], loc.at[4]),
    ]
    for d in own:
        d.start()
    st[...] = jnp.zeros_like(st)
    pl.semaphore_wait(barrier, (NT - 1) + (NY - 1) + (NZ - 1))

    def ti(j):
        return lax.rem(t + j, NT)

    yb, yf, y2 = yi(-turn), yi(turn), yi(2)

    class RowGather:
        def __init__(self, buf, ss, rs, first):
            self.buf, self.ss, self.rs = buf, ss, rs
            self.put(first, t, 0, NC * xi(1) + c)
            self.put(first, t, 1, NC * xi(-1) + c)
            self.put(first, t, 2, NC * x + sib)

        def put(self, src, slot, k, to):
            send(src, self.buf.at[slot], self.ss.at[k], self.rs.at[slot], dev(t_=to))

        def got(self, slot):
            arrived(self.buf.at[slot], self.ss.at[0], self.rs.at[slot])

        def forward(self):
            xb, xf = NC * xi(-turn) + c, NC * xi(turn) + c
            self.got(xb)
            self.put(self.buf.at[xb], xb, 3, xf)
            self.put(self.buf.at[xb], xb, 4, NC * x + sib)
            self.got(xf)
            self.put(self.buf.at[xf], xf, 5, NC * x + sib)

        def last(self):
            x2 = NC * xi(2) + c
            self.got(x2)
            self.put(self.buf.at[x2], x2, 6, NC * x + sib)

        def finish(self):
            for j in range(NX):
                self.got(NC * xi(j) + sib)

    class DepthRing:
        def __init__(self, block, ss, rs):
            self.block, self.ss, self.rs = block, ss, rs
            self.put(z, 0, zi(turn))
            self.put(z, 1, zi(-turn))

        def put(self, zz, k, to):
            r = self.block(zz)
            send(r, r, self.ss.at[k], self.rs.at[zz], dev(z_=to))

        def got(self, zz):
            arrived(self.block(zz), self.ss.at[0], self.rs.at[zz])

        def far(self, h):
            zz = zi(-h * turn)
            self.got(zz)
            if h < 4:
                self.put(zz, 2 * h, zi(turn))
            return zz

        def near(self, h):
            zz = zi(h * turn)
            self.got(zz)
            if h < 3:
                self.put(zz, 2 * h + 1, zi(-turn))
            return zz

    for h in range(2):
        for j in (4, 5, 3, 2, 6, 1, 7):
            to = ti(j)
            send(att.at[h, to], s1.at[h, t], a1s.at[h, j], a1r.at[h, t], dev(t_=to))
    for j in (4, 5, 3, 2, 6, 1, 7):
        to = ti(j)
        send(proj.at[to, z], pb.at[z, t], pxs.at[j], pxr.at[t], dev(t_=to))
    mine = []
    for h in range(2):
        own[h].wait()
        for j in range(1, NT):
            s = ti(j)
            arrived(s1.at[h, s], a1s.at[h, 0], a1r.at[h, s])
        for j in (2, 1, 3):
            q = yi(j)
            send(s1.at[h, pl.ds(2 * q, 2)], ab.at[h, t, y], b1s.at[h, j], b1r.at[h, y], dev(y_=q))
        mine.append(
            pltpu.make_async_copy(s1.at[h, pl.ds(2 * y, 2)], ab.at[h, t, y], loc.at[5 + h])
        )
        mine[h].start()
    send(cot, cb.at[y], cys.at[0], cyr.at[y], dev(y_=yi(1)))
    send(cot, cb.at[y], cys.at[1], cyr.at[y], dev(y_=yi(-1)))

    def row_ready(h):
        for j in range(1, NY):
            q = yi(j)
            arrived(ab.at[h, t, q], b1s.at[h, 0], b1r.at[h, q])
        mine[h].wait()
        return RowGather(ab.at[h], c1s.at[h], c1r.at[h], ab.at[h, t])

    rows0 = row_ready(0)
    own[4].wait()
    for j in range(1, NT):
        k = ti(j)
        arrived(pb.at[z, k], pxs.at[0], pxr.at[k])
    depth = [
        DepthRing(lambda zz, b=b: pb.at[zz, 4 * b : 4 * b + 4], pzs.at[b], pzr.at[b])
        for b in range(2)
    ]
    rows1 = row_ready(1)
    rows0.forward()
    arrived(cb.at[yb], cys.at[0], cyr.at[yb])
    send(cb.at[yb], cb.at[yb], cys.at[2], cyr.at[yb], dev(y_=yf))
    for d in depth:
        d.far(1)
        d.near(1)
    rows1.forward()
    rows0.last()
    for d in depth:
        d.far(2)
        d.near(2)
    rows0.finish()

    def grad(h):
        def one(i, _):
            r, b = lax.div(i, 2), lax.rem(i, 2)
            a = ab[h, :, r, b].reshape(256, 512)
            v = lax.dot_general(
                cb[r, 256 * h : 256 * (h + 1), :],
                a,
                (((0,), (0,)), ((), ())),
                preferred_element_type=F32,
            )
            for k in range(4):
                u = v[:, 128 * k : 128 * (k + 1)]
                g[r, 4 * b + k] = u if h == 0 else g[r, 4 * b + k] + u
            return 0

        lax.fori_loop(0, 8, one, 0)

    own[2].wait()
    arrived(cb.at[yf], cys.at[0], cyr.at[yf])
    arrived(cb.at[y2], cys.at[0], cyr.at[y2])
    grad(0)
    rows1.last()
    for d in depth:
        d.far(3)
    rows1.finish()
    grad(1)

    def dots(load, n, steps, top):
        pn = pairs(n)

        def one(i, acc):
            v = [load(k, i) for k in range(n)]
            new = [a + v[p] * v[q] for a, (p, q) in zip(acc, pn)]
            if top:
                new += [jnp.maximum(a, jnp.abs(u)) for a, u in zip(acc[len(pn) :], v)]
            return tuple(new)

        size = len(pn) + (n if top else 0)
        acc = lax.fori_loop(
            0, steps, one, tuple(jnp.zeros((8, 128), F32) for _ in range(size)), unroll=2
        )
        for k, a in enumerate(acc[: len(pn)]):
            st[k : k + 1, :] = jnp.sum(a, axis=0, keepdims=True)
        for k, a in enumerate(acc[len(pn) :]):
            m = jnp.max(jnp.max(a, axis=0, keepdims=True), axis=1, keepdims=True)
            st[len(pn) + k : len(pn) + k + 1, :] = jnp.broadcast_to(m * (1.0 / 128), (1, 128))
        row = jnp.sum(jnp.transpose(st[...]), axis=0, keepdims=True)
        return jnp.broadcast_to(row, (8, 128))

    def load_g(k, i):
        return g[k, lax.div(i, 32), pl.ds(pl.multiple_of(lax.rem(i, 32) * 8, 8), 8), :]

    local = dots(load_g, NY, 256, False)

    def share(buf, slot, ss, rs, count, index, where):
        for j in range(1, count):
            send(buf.at[slot], buf.at[slot], ss.at[j], rs.at[slot], where(index(j)))
        for j in range(1, count):
            k = index(j)
            arrived(buf.at[k], ss.at[0], rs.at[k])
        total = buf[0]
        for k in range(1, count):
            total = total + buf[k]
        return total

    def spread(total, n):
        return [jnp.broadcast_to(total[0:1, k : k + 1], (1, 128)) for k in range(n)]

    def plane(j):
        return lax.rem(y * NT + t + j, NY * NT)

    me = y * NT + t
    sr[me] = local
    total = share(
        sr,
        me,
        g1s,
        g1r,
        NY * NT,
        plane,
        lambda k: dev(y_=lax.div(k, NT), t_=lax.rem(k, NT)),
    )
    cots = RowGather(cf, cfs, cfr, cot)
    w = tree_weights(spread(total, 10), NY)

    def merge_into(dst, load, ws):
        def one(i, top):
            at = pl.ds(pl.multiple_of(i * 8, 8), 8)
            v = load(0, at) * ws[0]
            for k in range(1, len(ws)):
                v = v + load(k, at) * ws[k]
            dst[at, :] = v
            return jnp.maximum(top, jnp.abs(v))

        top = lax.fori_loop(0, 32, one, jnp.zeros((8, 128), F32), unroll=2)
        return jnp.max(jnp.max(top, axis=0, keepdims=True), axis=1, keepdims=True)

    for j in (4, 3, 5, 2, 6, 1, 7, 0):
        zz = zi(j)
        top = merge_into(
            rz.at[z] if j == 0 else mz.at[zz], lambda k, at, zz=zz: g[k, zz, at, :], w
        )
        if j:
            scale = jnp.broadcast_to(jnp.maximum(top, 1e-30), (16, 128)).astype(BF16)
            qz[zz, 256:272, :] = scale
            inv = 1.0 / scale[0:1, :].astype(F32)

            def code(i, _, zz=zz, inv=inv):
                at = pl.ds(pl.multiple_of(i * 16, 16), 16)
                qz[zz, at, :] = encode(mz[zz, at, :], inv, MU_Z)
                return 0

            lax.fori_loop(0, 16, code, 0, unroll=2)
            send(qz.at[zz], rq.at[z], zs.at[j], zr.at[z], dev(z_=zz))

    cots.forward()
    cots.last()
    for d in depth:
        d.near(3)
        d.far(4)
    own[3].wait()
    cots.finish()

    def part(i, _):
        k0, k1 = lax.div(i, 4), lax.rem(i, 4)
        at = pl.ds(pl.multiple_of(k0 * 256, 256), 256)
        v = jnp.zeros((256, 128), F32)
        for k in range(NT):
            b = pb[pl.ds(2 * k1, 2), k].reshape(128, 256)
            v = v + lax.dot_general(
                cf[k, at, :], b, (((1,), (1,)), ((), ())), preferred_element_type=F32
            )
        igrad[at, pl.ds(pl.multiple_of(k1 * 128, 128), 128)] = v.astype(BF16)
        return 0

    lax.fori_loop(0, 8, part, 0)

    for j in (1, 7, 2, 6, 3, 5, 4):
        k = zi(j)
        arrived(rq.at[k], zs.at[0], zr.at[k])
        scale = rq[k, 256:272, :].astype(F32)

        def uncode(i, _, k=k, scale=scale):
            at = pl.ds(pl.multiple_of(i * 16, 16), 16)
            rz[k, at, :] = decode(rq[k, at, :], scale, MU_Z)
            return 0

        lax.fori_loop(0, 16, uncode, 0, unroll=2)

    def load_r(k, i):
        return rz[k, pl.ds(pl.multiple_of(i * 8, 8), 8), :]

    tr1[t] = dots(load_r, NZ, 32, True)
    tr2[dp] = share(tr1, t, h1s, h1r, NT, ti, lambda k: dev(t_=k))
    total = share(
        tr2,
        dp,
        h2s,
        h2r,
        NY * NZ,
        lambda j: lax.rem(dp + j, NY * NZ),
        lambda k: {"dp": k, "tensor": t},
    )
    rows = spread(total, 44)
    w = tree_weights(rows, NZ)
    merge_into(mz.at[z], lambda k, at: rz[k, at, :], w)
    scale = jnp.full((1, 128), 1e-30, F32)
    for k in range(NZ):
        scale = scale + jnp.abs(w[k]) * rows[36 + k]
    scale = scale[0:1, 0:1]
    inv = 1.0 / scale
    mt[...] = jnp.transpose(mz[z])

    def code(i, _):
        at = pl.ds(pl.multiple_of(i * 16, 16), 16)
        fc[y, z, at, :] = encode(mt[at, :], inv, MU_F)
        return 0

    lax.fori_loop(0, 8, code, 0, unroll=2)

    def show(yy, zz, low):
        def one(i, _):
            at = pl.ds(pl.multiple_of(i * 16, 16), 16)
            fin[yy, zz, at, :] = decode(fc[yy, zz, at, :], scale, MU_F)
            return 0

        lo, hi = (CUT // 16, 8) if low else (0, CUT // 16)
        lax.fori_loop(lo, hi, one, 0, unroll=2)

    upper, lower = pl.ds(0, CUT), pl.ds(CUT, 128 - CUT)

    def f1z_got(zz):
        arrived(fc.at[y, zz, upper], f1zs.at[0], f1zr.at[zz])

    def f1y(yy, zz, k, to):
        r = fc.at[yy, zz, upper]
        send(r, r, f1ys.at[k, zz], f1yr.at[yy, zz], dev(y_=to))

    def f1y_got(yy, zz):
        arrived(fc.at[yy, zz, upper], f1ys.at[0, 0], f1yr.at[yy, zz])

    def f1y_start(zz):
        f1y(y, zz, 0, yf)
        f1y(y, zz, 1, yb)
        show(y, zz, False)

    def f1y_forward(zz):
        f1y_got(yb, zz)
        f1y(yb, zz, 2, yf)
        show(yb, zz, False)

    def f2z(zz, k, to):
        r = fc.at[:, zz, lower]
        send(r, r, f2zs.at[k], f2zr.at[zz], dev(z_=to))

    def f2z_got(zz):
        arrived(fc.at[:, zz, lower], f2zs.at[0], f2zr.at[zz])

    r = fc.at[y, z, lower]
    for j in (2, 1, 3):
        send(r, r, f2ys.at[j], f2yr.at[y], dev(y_=yi(j)))
    r = fc.at[y, z, upper]
    for j in (1, 7, 2, 6, 3, 5, 4):
        send(r, r, f1zs.at[j], f1zr.at[z], dev(z_=zi(j)))
    f1y_start(z)
    for j in range(1, NY):
        k = yi(j)
        arrived(fc.at[k, z, lower], f2ys.at[0], f2yr.at[k])
    f2z(z, 0, zi(turn))
    f2z(z, 1, zi(-turn))
    f2z(z, 2, zi(2 * turn))
    f2z(z, 3, zi(-2 * turn))

    def start(*js):
        for j in js:
            f1z_got(zi(j))
            f1y_start(zi(j))

    start(1, 7)
    f1y_forward(z)
    start(2, 6)
    f2z_got(zi(-2 * turn))
    f2z(zi(-2 * turn), 4, zi(2 * turn))
    f2z(zi(-2 * turn), 5, zi(turn))
    f2z_got(zi(2 * turn))
    f2z(zi(2 * turn), 6, zi(-turn))
    f1y_forward(zi(1))
    f1y_forward(zi(7))
    start(3, 5)
    f1y_forward(zi(2))
    f1y_forward(zi(6))
    start(4)
    for j in (3, 5, 4):
        f1y_forward(zi(j))
    for k in range(NY):
        show(k, z, True)
    for j in (2, 6):
        for k in range(NY):
            show(k, zi(j), True)
    for j in (0, 1, 7, 2, 6, 3, 5, 4):
        zz = zi(j)
        f1y_got(yf, zz)
        show(yf, zz, False)
        f1y_got(y2, zz)
        show(y2, zz, False)
        if j in (1, 7, 3, 5, 4):
            f2z_got(zz)
            for k in range(NY):
                show(k, zz, True)
    for d in sent:
        d.wait_send()


def on_device(attention, cotangent, projection):
    dma = pltpu.SemaphoreType.DMA

    def hbm(a):
        return pltpu.with_memory_space_constraint(a, pltpu.HBM)

    v = pltpu.VMEM
    igrad, comb = pl.pallas_call(
        body,
        out_shape=(
            jax.ShapeDtypeStruct((512, 512), BF16),
            jax.ShapeDtypeStruct((NY, NZ, 128, 256), F32),
        ),
        in_specs=[pl.BlockSpec(memory_space=pl.ANY)] * 3,
        out_specs=(
            pl.BlockSpec(memory_space=pltpu.VMEM),
            pl.BlockSpec(memory_space=pltpu.VMEM),
        ),
        scratch_shapes=[
            v((2, NT, 32, 512), BF16),
            v((2, NT, NY, 2, 32, 512), BF16),
            v((NY, 512, 256), BF16),
            v((NT, 512, 256), BF16),
            v((NZ, NT, 64, 256), BF16),
            v((NY, NZ, 256, 128), F32),
            v((NZ, 256, 128), F32),
            v((NZ, 256, 128), F32),
            v((NZ, 272, 128), BF16),
            v((NZ, 272, 128), BF16),
            v((NY, NZ, 128, 256), BF16),
            v((128, 256), F32),
            v((128, 128), F32),
            v((NY * NT, 8, 128), F32),
            v((NT, 8, 128), F32),
            v((NY * NZ, 8, 128), F32),
            dma((7,)),
            dma((2, NT)),
            dma((2, NT)),
            dma((2, NY)),
            dma((2, NY)),
            dma((2, 7)),
            dma((2, NT)),
            dma((3,)),
            dma((NY,)),
            dma((7,)),
            dma((NT,)),
            dma((NT,)),
            dma((NT,)),
            dma((2, 8)),
            dma((2, NZ)),
            dma((NY * NT,)),
            dma((NY * NT,)),
            dma((NZ,)),
            dma((NZ,)),
            dma((NT,)),
            dma((NT,)),
            dma((NY * NZ,)),
            dma((NY * NZ,)),
            dma((NZ,)),
            dma((NZ,)),
            dma((3, NZ)),
            dma((NY, NZ)),
            dma((NY,)),
            dma((NY,)),
            dma((7,)),
            dma((NZ,)),
        ],
        compiler_params=pltpu.CompilerParams(
            collective_id=0, has_side_effects=True, vmem_limit_bytes=48 * 1024 * 1024
        ),
        cost_estimate=pl.CostEstimate(
            flops=4 * 2**30, bytes_accessed=16 * 2**20, transcendentals=0
        ),
    )(
        hbm(attention.reshape(2, NT, 32, 512)),
        hbm(cotangent),
        hbm(projection.reshape(NT, NZ, 64, 256)),
    )
    return (igrad, comb.reshape(4096, 256))


def solution(mesh):
    return jax.shard_map(
        on_device,
        mesh=mesh,
        in_specs=(P("dp", "tensor"), P("dp", "tensor"), P(None, "tensor")),
        out_specs=(P("dp", "tensor"), P(None, "tensor")),
        check_vma=False,
    )
```

```python
import math

import jax
import jax.numpy as jnp
from jax import lax
from jax.experimental import pallas as pl
from jax.experimental.pallas import tpu as pltpu
from jax.sharding import PartitionSpec as P

EPS = 1e-06
MESH = pl.DeviceIdType.MESH
NX, NC, NY, NZ = 4, 2, 4, 8
NT = NX * NC
F32 = jnp.float32
BF16 = jnp.bfloat16
CUT = 112


MU_Z = 2.0**8 - 1
MU_F = 2.0**12 - 1
TOP = 125.0
H = 4


def encode(v, inv, mu):
    k = jnp.log(1.0 + jnp.abs(v) * (inv * mu)) * (2 * TOP / math.log(1.0 + mu)) - TOP
    e = jnp.exp2(k)
    return jnp.where(v < 0, -e, e).astype(BF16)


def decode(q, scale, mu):
    q = q.astype(F32)
    a = math.log(1.0 + mu) / (2 * TOP)
    h = jnp.log(jnp.abs(q)) * (a / math.log(2.0)) + TOP * a
    u = (jnp.exp(h) - 1.0) * (scale * (1.0 / mu))
    return jnp.where(q < 0, -u, u)


def pairs(n):
    return [(i, j) for i in range(n) for j in range(i, n)]


def tree_weights(rows, n):
    table = {}
    for k, (i, j) in enumerate(pairs(n)):
        table[i, j] = table[j, i] = rows[k]
    weights = [None] * n
    span, m = 1, n
    while m > 1:
        half = m // 2
        coef = []
        for i in range(half):
            aa = jnp.maximum(table[2 * i, 2 * i], 0.0)
            bb = jnp.maximum(table[2 * i + 1, 2 * i + 1], 0.0)
            s = table[2 * i, 2 * i + 1]
            coef.append(1.0 - s / (2.0 * (aa + EPS)))
            coef.append(1.0 - s / (2.0 * (bb + EPS)))
        for k in range(n):
            c = coef[k // span]
            weights[k] = c if weights[k] is None else weights[k] * c
        if half > 1:
            new = {}
            for i in range(half):
                for j in range(i, half):
                    if i == j:
                        a, b = 2 * i, 2 * i + 1
                        v = (
                            coef[a] * coef[a] * table[a, a]
                            + coef[b] * coef[b] * table[b, b]
                            + 2.0 * (coef[a] * coef[b] * table[a, b])
                        )
                    else:
                        v = coef[2 * i] * (
                            coef[2 * j] * table[2 * i, 2 * j]
                            + coef[2 * j + 1] * table[2 * i, 2 * j + 1]
                        ) + coef[2 * i + 1] * (
                            coef[2 * j] * table[2 * i + 1, 2 * j]
                            + coef[2 * j + 1] * table[2 * i + 1, 2 * j + 1]
                        )
                    new[i, j] = new[j, i] = v
            table = new
        span, m = span * 2, half
    return weights


def body(
    att,
    cot,
    proj,
    igrad,
    fin,
    s1,
    ab,
    cb,
    cf,
    pb,
    g,
    mz,
    rz,
    qz,
    rq,
    fc,
    mt,
    st,
    sr,
    tr1,
    tr2,
    loc,
    a1s,
    a1r,
    b1s,
    b1r,
    c1s,
    c1r,
    cys,
    cyr,
    cfs,
    cfr,
    pxs,
    pxr,
    pzs,
    pzr,
    g1s,
    g1r,
    zs,
    zr,
    h1s,
    h1r,
    h2s,
    h2r,
    f1zs,
    f1zr,
    f1ys,
    f1yr,
    f2ys,
    f2yr,
    f2zs,
    f2zr,
):
    dp = lax.axis_index("dp")
    t = lax.axis_index("tensor")
    z, y = lax.div(dp, NY), lax.rem(dp, NY)
    x, c = lax.div(t, NC), lax.rem(t, NC)
    turn = 1 - 2 * c
    sib = 1 - c

    def xi(d):
        return lax.rem(x + d + NX, NX)

    def yi(d):
        return lax.rem(y + d + NY, NY)

    def zi(d):
        return lax.rem(z + d + NZ, NZ)

    def dev(z_=None, y_=None, t_=None):
        z_ = z if z_ is None else z_
        y_ = y if y_ is None else y_
        t_ = t if t_ is None else t_
        return {"dp": z_ * NY + y_, "tensor": t_}

    def copy(src, dst, ss, rs, to):
        return pltpu.make_async_remote_copy(
            src_ref=src, dst_ref=dst, send_sem=ss, recv_sem=rs, device_id=to, device_id_type=MESH
        )

    sent = []

    def send(src, dst, ss, rs, to):
        d = copy(src, dst, ss, rs, to)
        d.start()
        sent.append(d)

    def arrived(ref, ss, rs):
        copy(ref, ref, ss, rs, dev()).wait_recv()

    barrier = pltpu.get_barrier_semaphore()
    for j in range(1, NT):
        pl.semaphore_signal(barrier, 1, device_id=dev(t_=lax.rem(t + j, NT)), device_id_type=MESH)
    for j in range(1, NY):
        pl.semaphore_signal(barrier, 1, device_id=dev(y_=yi(j)), device_id_type=MESH)
    for j in range(1, NZ):
        pl.semaphore_signal(barrier, 1, device_id=dev(z_=zi(j)), device_id_type=MESH)
    own = [
        pltpu.make_async_copy(att.at[:, t], s1.at[:, t], loc.at[0]),
        pltpu.make_async_copy(cot, cb.at[y], loc.at[1]),
        pltpu.make_async_copy(cot, cf.at[t], loc.at[2]),
        pltpu.make_async_copy(proj.at[t, z], pb.at[z, t], loc.at[3]),
    ]
    for d in own:
        d.start()
    st[...] = jnp.zeros_like(st)
    pl.semaphore_wait(barrier, (NT - 1) + (NY - 1) + (NZ - 1))

    def ti(j):
        return lax.rem(t + j, NT)

    yb, yf, y2 = yi(-turn), yi(turn), yi(2)

    class RowGather:
        def __init__(self, buf, ss, rs, first):
            self.buf, self.ss, self.rs = buf, ss, rs
            self.put(first, t, 0, NC * xi(1) + c)
            self.put(first, t, 1, NC * xi(-1) + c)
            self.put(first, t, 2, NC * x + sib)

        def put(self, src, slot, k, to):
            send(src, self.buf.at[slot], self.ss.at[k], self.rs.at[slot], dev(t_=to))

        def got(self, slot):
            arrived(self.buf.at[slot], self.ss.at[0], self.rs.at[slot])

        def forward(self):
            xb, xf = NC * xi(-turn) + c, NC * xi(turn) + c
            self.got(xb)
            self.put(self.buf.at[xb], xb, 3, xf)
            self.put(self.buf.at[xb], xb, 4, NC * x + sib)
            self.got(xf)
            self.put(self.buf.at[xf], xf, 5, NC * x + sib)

        def last(self):
            x2 = NC * xi(2) + c
            self.got(x2)
            self.put(self.buf.at[x2], x2, 6, NC * x + sib)

        def finish(self):
            for j in range(NX):
                self.got(NC * xi(j) + sib)

    class DepthRing:
        def __init__(self, block, ss, rs):
            self.block, self.ss, self.rs = block, ss, rs
            self.put(z, 0, zi(turn))
            self.put(z, 1, zi(-turn))

        def put(self, zz, k, to):
            r = self.block(zz)
            send(r, r, self.ss.at[k], self.rs.at[zz], dev(z_=to))

        def got(self, zz):
            arrived(self.block(zz), self.ss.at[0], self.rs.at[zz])

        def far(self, h):
            zz = zi(-h * turn)
            self.got(zz)
            if h < 4:
                self.put(zz, 2 * h, zi(turn))
            return zz

        def near(self, h):
            zz = zi(h * turn)
            self.got(zz)
            if h < 3:
                self.put(zz, 2 * h + 1, zi(-turn))
            return zz

    for h in range(H):
        for j in (4, 5, 3, 2, 6, 1, 7):
            to = ti(j)
            send(att.at[h, to], s1.at[h, t], a1s.at[h, j], a1r.at[h, t], dev(t_=to))
    for j in (4, 5, 3, 2, 6, 1, 7):
        to = ti(j)
        send(proj.at[to, z], pb.at[z, t], pxs.at[j], pxr.at[t], dev(t_=to))
    mine = []
    own[0].wait()
    for h in range(H):
        for j in range(1, NT):
            s = ti(j)
            arrived(s1.at[h, s], a1s.at[h, 0], a1r.at[h, s])
        for j in (2, 1, 3):
            q = yi(j)
            send(s1.at[h, pl.ds(2 * q, 2)], ab.at[h, t, y], b1s.at[h, j], b1r.at[h, y], dev(y_=q))
        mine.append(
            pltpu.make_async_copy(s1.at[h, pl.ds(2 * y, 2)], ab.at[h, t, y], loc.at[4 + h])
        )
        mine[h].start()
    send(cot, cb.at[y], cys.at[0], cyr.at[y], dev(y_=yi(1)))
    send(cot, cb.at[y], cys.at[1], cyr.at[y], dev(y_=yi(-1)))

    def row_ready(h):
        for j in range(1, NY):
            q = yi(j)
            arrived(ab.at[h, t, q], b1s.at[h, 0], b1r.at[h, q])
        mine[h].wait()
        return RowGather(ab.at[h], c1s.at[h], c1r.at[h], ab.at[h, t])

    rows = [row_ready(0), row_ready(1)]
    own[3].wait()
    for j in range(1, NT):
        k = ti(j)
        arrived(pb.at[z, k], pxs.at[0], pxr.at[k])
    depth = [
        DepthRing(lambda zz, b=b: pb.at[zz, 4 * b : 4 * b + 4], pzs.at[b], pzr.at[b])
        for b in range(2)
    ]
    rows.append(row_ready(2))
    rows[0].forward()
    rows.append(row_ready(3))
    rows[1].forward()
    arrived(cb.at[yb], cys.at[0], cyr.at[yb])
    send(cb.at[yb], cb.at[yb], cys.at[2], cyr.at[yb], dev(y_=yf))
    for d in depth:
        d.far(1)
        d.near(1)
    rows[0].last()
    rows[2].forward()
    rows[1].last()
    rows[3].forward()
    for d in depth:
        d.far(2)
        d.near(2)
    rows[2].last()
    rows[0].finish()
    rows[1].finish()

    def grad(h):
        def one(i, _):
            r, b = lax.div(i, 2), lax.rem(i, 2)
            a = ab[2 * h : 2 * h + 2, :, r, b].reshape(256, 512)
            v = lax.dot_general(
                cb[r, 256 * h : 256 * (h + 1), :],
                a,
                (((0,), (0,)), ((), ())),
                preferred_element_type=F32,
            )
            for k in range(4):
                u = v[:, 128 * k : 128 * (k + 1)]
                g[r, 4 * b + k] = u if h == 0 else g[r, 4 * b + k] + u
            return 0

        lax.fori_loop(0, 8, one, 0)

    own[1].wait()
    arrived(cb.at[yf], cys.at[0], cyr.at[yf])
    arrived(cb.at[y2], cys.at[0], cyr.at[y2])
    grad(0)
    rows[3].last()
    for d in depth:
        d.far(3)
    rows[2].finish()
    rows[3].finish()
    grad(1)

    def dots(load, n, steps, top):
        pn = pairs(n)

        def one(i, acc):
            v = [load(k, i) for k in range(n)]
            new = [a + v[p] * v[q] for a, (p, q) in zip(acc, pn)]
            if top:
                new += [jnp.maximum(a, jnp.abs(u)) for a, u in zip(acc[len(pn) :], v)]
            return tuple(new)

        size = len(pn) + (n if top else 0)
        acc = lax.fori_loop(
            0, steps, one, tuple(jnp.zeros((8, 128), F32) for _ in range(size)), unroll=2
        )
        for k, a in enumerate(acc[: len(pn)]):
            st[k : k + 1, :] = jnp.sum(a, axis=0, keepdims=True)
        for k, a in enumerate(acc[len(pn) :]):
            m = jnp.max(jnp.max(a, axis=0, keepdims=True), axis=1, keepdims=True)
            st[len(pn) + k : len(pn) + k + 1, :] = jnp.broadcast_to(m * (1.0 / 128), (1, 128))
        row = jnp.sum(jnp.transpose(st[...]), axis=0, keepdims=True)
        return jnp.broadcast_to(row, (8, 128))

    def load_g(k, i):
        return g[k, lax.div(i, 32), pl.ds(pl.multiple_of(lax.rem(i, 32) * 8, 8), 8), :]

    local = dots(load_g, NY, 256, False)

    lane = lax.broadcasted_iota(jnp.int32, (8, 128), 1)
    maxima = lane >= len(pairs(NZ))

    def share(buf, slot, ss, rs, count, index, where, meanwhile=None):
        for j in range(1, count):
            send(buf.at[slot], buf.at[slot], ss.at[j], rs.at[slot], where(index(j)))
        if meanwhile is not None:
            meanwhile()
        for j in range(1, count):
            k = index(j)
            arrived(buf.at[k], ss.at[0], rs.at[k])
        total = top = buf[0]
        for k in range(1, count):
            total = total + buf[k]
            top = jnp.maximum(top, buf[k])
        return jnp.where(maxima, top, total)

    def spread(total, n):
        return [jnp.broadcast_to(total[0:1, k : k + 1], (1, 128)) for k in range(n)]

    def plane(j):
        return lax.rem(y * NT + t + j, NY * NT)

    me = y * NT + t
    sr[me] = local
    total = share(
        sr,
        me,
        g1s,
        g1r,
        NY * NT,
        plane,
        lambda k: dev(y_=lax.div(k, NT), t_=lax.rem(k, NT)),
    )
    cots = RowGather(cf, cfs, cfr, cot)
    w = tree_weights(spread(total, 10), NY)

    def merge_into(dst, load, ws):
        def one(i, top):
            at = pl.ds(pl.multiple_of(i * 8, 8), 8)
            v = load(0, at) * ws[0]
            for k in range(1, len(ws)):
                v = v + load(k, at) * ws[k]
            dst[at, :] = v
            return jnp.maximum(top, jnp.abs(v))

        top = lax.fori_loop(0, 32, one, jnp.zeros((8, 128), F32), unroll=2)
        return jnp.max(jnp.max(top, axis=0, keepdims=True), axis=1, keepdims=True)

    for j in (4, 3, 5, 2, 6, 1, 7, 0):
        zz = zi(j)
        top = merge_into(
            rz.at[z] if j == 0 else mz.at[zz], lambda k, at, zz=zz: g[k, zz, at, :], w
        )
        if j:
            scale = jnp.broadcast_to(jnp.maximum(top, 1e-30), (16, 128)).astype(BF16)
            qz[zz, 256:272, :] = scale
            inv = 1.0 / scale[0:1, :].astype(F32)

            def code(i, _, zz=zz, inv=inv):
                at = pl.ds(pl.multiple_of(i * 16, 16), 16)
                qz[zz, at, :] = encode(mz[zz, at, :], inv, MU_Z)
                return 0

            lax.fori_loop(0, 16, code, 0, unroll=2)
            send(qz.at[zz], rq.at[z], zs.at[j], zr.at[z], dev(z_=zz))

    cots.forward()
    for j in (1, 7, 2, 6, 3, 5, 4):
        k = zi(j)
        arrived(rq.at[k], zs.at[0], zr.at[k])
        scale = rq[k, 256:272, :].astype(F32)

        def uncode(i, _, k=k, scale=scale):
            at = pl.ds(pl.multiple_of(i * 16, 16), 16)
            rz[k, at, :] = decode(rq[k, at, :], scale, MU_Z)
            return 0

        lax.fori_loop(0, 16, uncode, 0, unroll=2)

    def load_r(k, i):
        return rz[k, pl.ds(pl.multiple_of(i * 8, 8), 8), :]

    cots.last()
    for d in depth:
        d.near(3)
        d.far(4)
    own[2].wait()

    def part(i, _):
        k0, k1 = lax.div(i, 4), lax.rem(i, 4)
        at = pl.ds(pl.multiple_of(k0 * 256, 256), 256)
        v = jnp.zeros((256, 128), F32)
        for k in range(NT):
            b = pb[pl.ds(2 * k1, 2), k].reshape(128, 256)
            v = v + lax.dot_general(
                cf[k, at, :], b, (((1,), (1,)), ((), ())), preferred_element_type=F32
            )
        igrad[at, pl.ds(pl.multiple_of(k1 * 128, 128), 128)] = v.astype(BF16)
        return 0

    def input_gradient():
        cots.finish()
        lax.fori_loop(0, 8, part, 0)

    tr1[t] = dots(load_r, NZ, 32, True)
    tr2[dp] = share(tr1, t, h1s, h1r, NT, ti, lambda k: dev(t_=k))
    total = share(
        tr2,
        dp,
        h2s,
        h2r,
        NY * NZ,
        lambda j: lax.rem(dp + j, NY * NZ),
        lambda k: {"dp": k, "tensor": t},
        input_gradient,
    )
    rows = spread(total, 44)
    w = tree_weights(rows, NZ)
    merge_into(mz.at[z], lambda k, at: rz[k, at, :], w)
    scale = jnp.full((1, 128), 1e-30, F32)
    for k in range(NZ):
        scale = scale + jnp.abs(w[k]) * rows[36 + k]
    scale = scale[0:1, 0:1]
    inv = 1.0 / scale
    mt[...] = jnp.transpose(mz[z])

    def code(i, _):
        at = pl.ds(pl.multiple_of(i * 16, 16), 16)
        fc[y, z, at, :] = encode(mt[at, :], inv, MU_F)
        return 0

    lax.fori_loop(0, 8, code, 0, unroll=2)

    def show(yy, zz, low):
        def one(i, _):
            at = pl.ds(pl.multiple_of(i * 16, 16), 16)
            fin[yy, zz, at, :] = decode(fc[yy, zz, at, :], scale, MU_F)
            return 0

        lo, hi = (CUT // 16, 8) if low else (0, CUT // 16)
        lax.fori_loop(lo, hi, one, 0, unroll=2)

    upper, lower = pl.ds(0, CUT), pl.ds(CUT, 128 - CUT)

    def f1z_got(zz):
        arrived(fc.at[y, zz, upper], f1zs.at[0], f1zr.at[zz])

    def f1y(yy, zz, k, to):
        r = fc.at[yy, zz, upper]
        send(r, r, f1ys.at[k, zz], f1yr.at[yy, zz], dev(y_=to))

    def f1y_got(yy, zz):
        arrived(fc.at[yy, zz, upper], f1ys.at[0, 0], f1yr.at[yy, zz])

    def f1y_start(zz):
        f1y(y, zz, 0, yf)
        f1y(y, zz, 1, yb)
        show(y, zz, False)

    def f1y_forward(zz):
        f1y_got(yb, zz)
        f1y(yb, zz, 2, yf)
        show(yb, zz, False)

    def f2z(zz, k, to):
        r = fc.at[:, zz, lower]
        send(r, r, f2zs.at[k], f2zr.at[zz], dev(z_=to))

    def f2z_got(zz):
        arrived(fc.at[:, zz, lower], f2zs.at[0], f2zr.at[zz])

    r = fc.at[y, z, lower]
    for j in (2, 1, 3):
        send(r, r, f2ys.at[j], f2yr.at[y], dev(y_=yi(j)))
    r = fc.at[y, z, upper]
    for j in (1, 7, 2, 6, 3, 5, 4):
        send(r, r, f1zs.at[j], f1zr.at[z], dev(z_=zi(j)))
    f1y_start(z)
    for j in range(1, NY):
        k = yi(j)
        arrived(fc.at[k, z, lower], f2ys.at[0], f2yr.at[k])
    f2z(z, 0, zi(turn))
    f2z(z, 1, zi(-turn))
    f2z(z, 2, zi(2 * turn))
    f2z(z, 3, zi(-2 * turn))

    def start(*js):
        for j in js:
            f1z_got(zi(j))
            f1y_start(zi(j))

    start(1, 7)
    f1y_forward(z)
    start(2, 6)
    f2z_got(zi(-2 * turn))
    f2z(zi(-2 * turn), 4, zi(2 * turn))
    f2z(zi(-2 * turn), 5, zi(turn))
    f2z_got(zi(2 * turn))
    f2z(zi(2 * turn), 6, zi(-turn))
    f1y_forward(zi(1))
    f1y_forward(zi(7))
    start(3, 5)
    f1y_forward(zi(2))
    f1y_forward(zi(6))
    start(4)
    for j in (3, 5, 4):
        f1y_forward(zi(j))
    for k in range(NY):
        show(k, z, True)
    for j in (2, 6):
        for k in range(NY):
            show(k, zi(j), True)
    for j in (0, 1, 7, 2, 6, 3, 5, 4):
        zz = zi(j)
        f1y_got(yf, zz)
        show(yf, zz, False)
        f1y_got(y2, zz)
        show(y2, zz, False)
        if j in (1, 7, 3, 5, 4):
            f2z_got(zz)
            for k in range(NY):
                show(k, zz, True)
    for d in sent:
        d.wait_send()


def on_device(attention, cotangent, projection):
    dma = pltpu.SemaphoreType.DMA

    def hbm(a):
        return pltpu.with_memory_space_constraint(a, pltpu.HBM)

    v = pltpu.VMEM
    igrad, comb = pl.pallas_call(
        body,
        out_shape=(
            jax.ShapeDtypeStruct((512, 512), BF16),
            jax.ShapeDtypeStruct((NY, NZ, 128, 256), F32),
        ),
        in_specs=[pl.BlockSpec(memory_space=pl.ANY)] * 3,
        out_specs=(
            pl.BlockSpec(memory_space=pltpu.VMEM),
            pl.BlockSpec(memory_space=pltpu.VMEM),
        ),
        scratch_shapes=[
            v((H, NT, 16, 512), BF16),
            v((H, NT, NY, 2, 16, 512), BF16),
            v((NY, 512, 256), BF16),
            v((NT, 512, 256), BF16),
            v((NZ, NT, 64, 256), BF16),
            v((NY, NZ, 256, 128), F32),
            v((NZ, 256, 128), F32),
            v((NZ, 256, 128), F32),
            v((NZ, 272, 128), BF16),
            v((NZ, 272, 128), BF16),
            v((NY, NZ, 128, 256), BF16),
            v((128, 256), F32),
            v((128, 128), F32),
            v((NY * NT, 8, 128), F32),
            v((NT, 8, 128), F32),
            v((NY * NZ, 8, 128), F32),
            dma((8,)),
            dma((H, NT)),
            dma((H, NT)),
            dma((H, NY)),
            dma((H, NY)),
            dma((H, 7)),
            dma((H, NT)),
            dma((3,)),
            dma((NY,)),
            dma((7,)),
            dma((NT,)),
            dma((NT,)),
            dma((NT,)),
            dma((2, 8)),
            dma((2, NZ)),
            dma((NY * NT,)),
            dma((NY * NT,)),
            dma((NZ,)),
            dma((NZ,)),
            dma((NT,)),
            dma((NT,)),
            dma((NY * NZ,)),
            dma((NY * NZ,)),
            dma((NZ,)),
            dma((NZ,)),
            dma((3, NZ)),
            dma((NY, NZ)),
            dma((NY,)),
            dma((NY,)),
            dma((7,)),
            dma((NZ,)),
        ],
        compiler_params=pltpu.CompilerParams(
            collective_id=0, has_side_effects=True, vmem_limit_bytes=48 * 1024 * 1024
        ),
        cost_estimate=pl.CostEstimate(
            flops=4 * 2**30, bytes_accessed=16 * 2**20, transcendentals=0
        ),
    )(
        hbm(attention.reshape(H, NT, 16, 512)),
        hbm(cotangent),
        hbm(projection.reshape(NT, NZ, 64, 256)),
    )
    return (igrad, comb.reshape(4096, 256))


def solution(mesh):
    return jax.shard_map(
        on_device,
        mesh=mesh,
        in_specs=(P("dp", "tensor"), P("dp", "tensor"), P(None, "tensor")),
        out_specs=(P("dp", "tensor"), P(None, "tensor")),
        check_vma=False,
    )
```

```python
import math

import jax
import jax.numpy as jnp
from jax import lax
from jax.experimental import pallas as pl
from jax.experimental.pallas import tpu as pltpu
from jax.sharding import PartitionSpec as P

EPS = 1e-06
MESH = pl.DeviceIdType.MESH
NX, NC, NY, NZ = 4, 2, 4, 8
NT = NX * NC
F32 = jnp.float32
BF16 = jnp.bfloat16
CUT = 112


MU_Z = 2.0**8 - 1
MU_F = 2.0**12 - 1
TOP = 125.0
H = 4


def encode(v, inv, mu):
    k = jnp.log(1.0 + jnp.abs(v) * (inv * mu)) * (2 * TOP / math.log(1.0 + mu)) - TOP
    e = jnp.exp2(k)
    return jnp.where(v < 0, -e, e).astype(BF16)


def decode(q, scale, mu):
    q = q.astype(F32)
    a = math.log(1.0 + mu) / (2 * TOP)
    h = jnp.log(jnp.abs(q)) * (a / math.log(2.0)) + TOP * a
    u = (jnp.exp(h) - 1.0) * (scale * (1.0 / mu))
    return jnp.where(q < 0, -u, u)


def pairs(n):
    return [(i, j) for i in range(n) for j in range(i, n)]


def tree_weights(rows, n):
    table = {}
    for k, (i, j) in enumerate(pairs(n)):
        table[i, j] = table[j, i] = rows[k]
    weights = [None] * n
    span, m = 1, n
    while m > 1:
        half = m // 2
        coef = []
        for i in range(half):
            aa = jnp.maximum(table[2 * i, 2 * i], 0.0)
            bb = jnp.maximum(table[2 * i + 1, 2 * i + 1], 0.0)
            s = table[2 * i, 2 * i + 1]
            coef.append(1.0 - s / (2.0 * (aa + EPS)))
            coef.append(1.0 - s / (2.0 * (bb + EPS)))
        for k in range(n):
            c = coef[k // span]
            weights[k] = c if weights[k] is None else weights[k] * c
        if half > 1:
            new = {}
            for i in range(half):
                for j in range(i, half):
                    if i == j:
                        a, b = 2 * i, 2 * i + 1
                        v = (
                            coef[a] * coef[a] * table[a, a]
                            + coef[b] * coef[b] * table[b, b]
                            + 2.0 * (coef[a] * coef[b] * table[a, b])
                        )
                    else:
                        v = coef[2 * i] * (
                            coef[2 * j] * table[2 * i, 2 * j]
                            + coef[2 * j + 1] * table[2 * i, 2 * j + 1]
                        ) + coef[2 * i + 1] * (
                            coef[2 * j] * table[2 * i + 1, 2 * j]
                            + coef[2 * j + 1] * table[2 * i + 1, 2 * j + 1]
                        )
                    new[i, j] = new[j, i] = v
            table = new
        span, m = span * 2, half
    return weights


def body(
    att,
    cot,
    proj,
    igrad,
    fin,
    s1,
    ab,
    cb,
    cf,
    pb,
    g,
    mz,
    rz,
    qz,
    rq,
    fc,
    mt,
    st,
    sr,
    tr1,
    tr2,
    loc,
    a1s,
    a1r,
    b1s,
    b1r,
    c1s,
    c1r,
    cys,
    cyr,
    cfs,
    cfr,
    pxs,
    pxr,
    g1s,
    g1r,
    zs,
    zr,
    h1s,
    h1r,
    h2s,
    h2r,
    f1zs,
    f1zr,
    f1ys,
    f1yr,
    f2ys,
    f2yr,
    f2zs,
    f2zr,
):
    dp = lax.axis_index("dp")
    t = lax.axis_index("tensor")
    z, y = lax.div(dp, NY), lax.rem(dp, NY)
    x, c = lax.div(t, NC), lax.rem(t, NC)
    turn = 1 - 2 * c
    sib = 1 - c

    def xi(d):
        return lax.rem(x + d + NX, NX)

    def yi(d):
        return lax.rem(y + d + NY, NY)

    def zi(d):
        return lax.rem(z + d + NZ, NZ)

    def dev(z_=None, y_=None, t_=None):
        z_ = z if z_ is None else z_
        y_ = y if y_ is None else y_
        t_ = t if t_ is None else t_
        return {"dp": z_ * NY + y_, "tensor": t_}

    def copy(src, dst, ss, rs, to):
        return pltpu.make_async_remote_copy(
            src_ref=src, dst_ref=dst, send_sem=ss, recv_sem=rs, device_id=to, device_id_type=MESH
        )

    sent = []

    def send(src, dst, ss, rs, to):
        d = copy(src, dst, ss, rs, to)
        d.start()
        sent.append(d)

    def arrived(ref, ss, rs):
        copy(ref, ref, ss, rs, dev()).wait_recv()

    barrier = pltpu.get_barrier_semaphore()
    for j in range(1, NT):
        pl.semaphore_signal(barrier, 1, device_id=dev(t_=lax.rem(t + j, NT)), device_id_type=MESH)
    for j in range(1, NY):
        pl.semaphore_signal(barrier, 1, device_id=dev(y_=yi(j)), device_id_type=MESH)
    for j in range(1, NZ):
        pl.semaphore_signal(barrier, 1, device_id=dev(z_=zi(j)), device_id_type=MESH)
    own = [
        pltpu.make_async_copy(att.at[:, t], s1.at[:, t], loc.at[0]),
        pltpu.make_async_copy(cot, cb.at[y], loc.at[1]),
        pltpu.make_async_copy(cot, cf.at[t], loc.at[2]),
        pltpu.make_async_copy(proj.at[t], pb.at[t], loc.at[3]),
    ]
    for d in own:
        d.start()
    st[...] = jnp.zeros_like(st)
    pl.semaphore_wait(barrier, (NT - 1) + (NY - 1) + (NZ - 1))

    def ti(j):
        return lax.rem(t + j, NT)

    yb, yf, y2 = yi(-turn), yi(turn), yi(2)

    class RowGather:
        def __init__(self, buf, ss, rs, first):
            self.buf, self.ss, self.rs = buf, ss, rs
            self.put(first, t, 0, NC * xi(1) + c)
            self.put(first, t, 1, NC * xi(-1) + c)
            self.put(first, t, 2, NC * x + sib)

        def put(self, src, slot, k, to):
            send(src, self.buf.at[slot], self.ss.at[k], self.rs.at[slot], dev(t_=to))

        def got(self, slot):
            arrived(self.buf.at[slot], self.ss.at[0], self.rs.at[slot])

        def forward(self):
            xb, xf = NC * xi(-turn) + c, NC * xi(turn) + c
            self.got(xb)
            self.put(self.buf.at[xb], xb, 3, xf)
            self.put(self.buf.at[xb], xb, 4, NC * x + sib)
            self.got(xf)
            self.put(self.buf.at[xf], xf, 5, NC * x + sib)

        def last(self):
            x2 = NC * xi(2) + c
            self.got(x2)
            self.put(self.buf.at[x2], x2, 6, NC * x + sib)

        def finish(self):
            for j in range(NX):
                self.got(NC * xi(j) + sib)

    for h in range(H):
        for j in (4, 5, 3, 2, 6, 1, 7):
            to = ti(j)
            send(att.at[h, to], s1.at[h, t], a1s.at[h, j], a1r.at[h, t], dev(t_=to))
    mine = []
    own[0].wait()
    for h in range(H):
        for j in range(1, NT):
            s = ti(j)
            arrived(s1.at[h, s], a1s.at[h, 0], a1r.at[h, s])
        for j in (2, 1, 3):
            q = yi(j)
            send(s1.at[h, pl.ds(2 * q, 2)], ab.at[h, t, y], b1s.at[h, j], b1r.at[h, y], dev(y_=q))
        mine.append(
            pltpu.make_async_copy(s1.at[h, pl.ds(2 * y, 2)], ab.at[h, t, y], loc.at[4 + h])
        )
        mine[h].start()
    send(cot, cb.at[y], cys.at[0], cyr.at[y], dev(y_=yi(1)))
    send(cot, cb.at[y], cys.at[1], cyr.at[y], dev(y_=yi(-1)))

    def row_ready(h):
        for j in range(1, NY):
            q = yi(j)
            arrived(ab.at[h, t, q], b1s.at[h, 0], b1r.at[h, q])
        mine[h].wait()
        return RowGather(ab.at[h], c1s.at[h], c1r.at[h], ab.at[h, t])

    rows = [row_ready(0), row_ready(1)]
    rows.append(row_ready(2))
    rows[0].forward()
    rows.append(row_ready(3))
    rows[1].forward()
    arrived(cb.at[yb], cys.at[0], cyr.at[yb])
    send(cb.at[yb], cb.at[yb], cys.at[2], cyr.at[yb], dev(y_=yf))
    rows[0].last()
    rows[2].forward()
    rows[1].last()
    rows[3].forward()
    rows[2].last()
    rows[0].finish()
    rows[1].finish()

    def grad(h):
        def one(i, _):
            r, b = lax.div(i, 2), lax.rem(i, 2)
            a = ab[2 * h : 2 * h + 2, :, r, b].reshape(256, 512)
            v = lax.dot_general(
                cb[r, 256 * h : 256 * (h + 1), :],
                a,
                (((0,), (0,)), ((), ())),
                preferred_element_type=F32,
            )
            for k in range(4):
                u = v[:, 128 * k : 128 * (k + 1)]
                g[r, 4 * b + k] = u if h == 0 else g[r, 4 * b + k] + u
            return 0

        lax.fori_loop(0, 8, one, 0)

    own[1].wait()
    arrived(cb.at[yf], cys.at[0], cyr.at[yf])
    arrived(cb.at[y2], cys.at[0], cyr.at[y2])
    grad(0)
    rows[3].last()
    rows[2].finish()
    rows[3].finish()
    grad(1)

    def dots(load, n, steps, top):
        pn = pairs(n)

        def one(i, acc):
            v = [load(k, i) for k in range(n)]
            new = [a + v[p] * v[q] for a, (p, q) in zip(acc, pn)]
            if top:
                new += [jnp.maximum(a, jnp.abs(u)) for a, u in zip(acc[len(pn) :], v)]
            return tuple(new)

        size = len(pn) + (n if top else 0)
        acc = lax.fori_loop(
            0, steps, one, tuple(jnp.zeros((8, 128), F32) for _ in range(size)), unroll=2
        )
        for k, a in enumerate(acc[: len(pn)]):
            st[k : k + 1, :] = jnp.sum(a, axis=0, keepdims=True)
        for k, a in enumerate(acc[len(pn) :]):
            m = jnp.max(jnp.max(a, axis=0, keepdims=True), axis=1, keepdims=True)
            st[len(pn) + k : len(pn) + k + 1, :] = jnp.broadcast_to(m * (1.0 / 128), (1, 128))
        row = jnp.sum(jnp.transpose(st[...]), axis=0, keepdims=True)
        return jnp.broadcast_to(row, (8, 128))

    def load_g(k, i):
        return g[k, lax.div(i, 32), pl.ds(pl.multiple_of(lax.rem(i, 32) * 8, 8), 8), :]

    local = dots(load_g, NY, 256, False)

    lane = lax.broadcasted_iota(jnp.int32, (8, 128), 1)
    maxima = lane >= len(pairs(NZ))

    def share(buf, slot, ss, rs, count, index, where, meanwhile=None):
        for j in range(1, count):
            send(buf.at[slot], buf.at[slot], ss.at[j], rs.at[slot], where(index(j)))
        if meanwhile is not None:
            meanwhile()
        for j in range(1, count):
            k = index(j)
            arrived(buf.at[k], ss.at[0], rs.at[k])
        total = top = buf[0]
        for k in range(1, count):
            total = total + buf[k]
            top = jnp.maximum(top, buf[k])
        return jnp.where(maxima, top, total)

    def spread(total, n):
        return [jnp.broadcast_to(total[0:1, k : k + 1], (1, 128)) for k in range(n)]

    def plane(j):
        return lax.rem(y * NT + t + j, NY * NT)

    me = y * NT + t
    sr[me] = local
    total = share(
        sr,
        me,
        g1s,
        g1r,
        NY * NT,
        plane,
        lambda k: dev(y_=lax.div(k, NT), t_=lax.rem(k, NT)),
    )
    cots = RowGather(cf, cfs, cfr, cot)
    w = tree_weights(spread(total, 10), NY)

    def merge_into(dst, load, ws):
        def one(i, top):
            at = pl.ds(pl.multiple_of(i * 8, 8), 8)
            v = load(0, at) * ws[0]
            for k in range(1, len(ws)):
                v = v + load(k, at) * ws[k]
            dst[at, :] = v
            return jnp.maximum(top, jnp.abs(v))

        top = lax.fori_loop(0, 32, one, jnp.zeros((8, 128), F32), unroll=2)
        return jnp.max(jnp.max(top, axis=0, keepdims=True), axis=1, keepdims=True)

    for j in (4, 3, 5, 2, 6, 1, 7, 0):
        zz = zi(j)
        top = merge_into(
            rz.at[z] if j == 0 else mz.at[zz], lambda k, at, zz=zz: g[k, zz, at, :], w
        )
        if j:
            scale = jnp.broadcast_to(jnp.maximum(top, 1e-30), (16, 128)).astype(BF16)
            qz[zz, 256:272, :] = scale
            inv = 1.0 / scale[0:1, :].astype(F32)

            def code(i, _, zz=zz, inv=inv):
                at = pl.ds(pl.multiple_of(i * 16, 16), 16)
                qz[zz, at, :] = encode(mz[zz, at, :], inv, MU_Z)
                return 0

            lax.fori_loop(0, 16, code, 0, unroll=2)
            send(qz.at[zz], rq.at[z], zs.at[j], zr.at[z], dev(z_=zz))

    cots.forward()
    for j in (1, 7, 2, 6, 3, 5, 4):
        k = zi(j)
        arrived(rq.at[k], zs.at[0], zr.at[k])
        scale = rq[k, 256:272, :].astype(F32)

        def uncode(i, _, k=k, scale=scale):
            at = pl.ds(pl.multiple_of(i * 16, 16), 16)
            rz[k, at, :] = decode(rq[k, at, :], scale, MU_Z)
            return 0

        lax.fori_loop(0, 16, uncode, 0, unroll=2)

    def load_r(k, i):
        return rz[k, pl.ds(pl.multiple_of(i * 8, 8), 8), :]

    cots.last()
    tr1[t] = dots(load_r, NZ, 32, True)
    tr2[dp] = share(tr1, t, h1s, h1r, NT, ti, lambda k: dev(t_=k))
    for j in (4, 5, 3, 2, 6, 1, 7):
        to = ti(j)
        send(proj.at[to], pb.at[t], pxs.at[j], pxr.at[t], dev(t_=to))
    total = share(
        tr2,
        dp,
        h2s,
        h2r,
        NY * NZ,
        lambda j: lax.rem(dp + j, NY * NZ),
        lambda k: {"dp": k, "tensor": t},
    )
    rows = spread(total, 44)
    w = tree_weights(rows, NZ)
    merge_into(mz.at[z], lambda k, at: rz[k, at, :], w)
    scale = jnp.full((1, 128), 1e-30, F32)
    for k in range(NZ):
        scale = scale + jnp.abs(w[k]) * rows[36 + k]
    scale = scale[0:1, 0:1]
    inv = 1.0 / scale
    mt[...] = jnp.transpose(mz[z])

    def code(i, _):
        at = pl.ds(pl.multiple_of(i * 16, 16), 16)
        fc[y, z, at, :] = encode(mt[at, :], inv, MU_F)
        return 0

    lax.fori_loop(0, 8, code, 0, unroll=2)

    def show(yy, zz, low):
        def one(i, _):
            at = pl.ds(pl.multiple_of(i * 16, 16), 16)
            fin[yy, zz, at, :] = decode(fc[yy, zz, at, :], scale, MU_F)
            return 0

        lo, hi = (CUT // 16, 8) if low else (0, CUT // 16)
        lax.fori_loop(lo, hi, one, 0, unroll=2)

    upper, lower = pl.ds(0, CUT), pl.ds(CUT, 128 - CUT)

    def f1z_got(zz):
        arrived(fc.at[y, zz, upper], f1zs.at[0], f1zr.at[zz])

    def f1y(yy, zz, k, to):
        r = fc.at[yy, zz, upper]
        send(r, r, f1ys.at[k, zz], f1yr.at[yy, zz], dev(y_=to))

    def f1y_got(yy, zz):
        arrived(fc.at[yy, zz, upper], f1ys.at[0, 0], f1yr.at[yy, zz])

    def f1y_start(zz):
        f1y(y, zz, 0, yf)
        f1y(y, zz, 1, yb)
        show(y, zz, False)

    def f1y_forward(zz):
        f1y_got(yb, zz)
        f1y(yb, zz, 2, yf)
        show(yb, zz, False)

    def f2z(zz, k, to):
        r = fc.at[:, zz, lower]
        send(r, r, f2zs.at[k], f2zr.at[zz], dev(z_=to))

    def f2z_got(zz):
        arrived(fc.at[:, zz, lower], f2zs.at[0], f2zr.at[zz])

    r = fc.at[y, z, lower]
    for j in (2, 1, 3):
        send(r, r, f2ys.at[j], f2yr.at[y], dev(y_=yi(j)))
    r = fc.at[y, z, upper]
    for j in (1, 7, 4, 3, 5, 2, 6):
        send(r, r, f1zs.at[j], f1zr.at[z], dev(z_=zi(j)))
    f1y_start(z)
    for j in range(1, NY):
        k = yi(j)
        arrived(fc.at[k, z, lower], f2ys.at[0], f2yr.at[k])
    f2z(z, 0, zi(turn))
    f2z(z, 1, zi(-turn))
    f2z(z, 2, zi(2 * turn))
    f2z(z, 3, zi(-2 * turn))

    def start(*js):
        for j in js:
            f1z_got(zi(j))
            f1y_start(zi(j))

    start(1, 7)
    f1y_forward(z)
    start(4)
    f1y_forward(zi(1))
    f1y_forward(zi(7))
    start(3, 5)
    f1y_forward(zi(4))
    for j in (2, 6):
        zz = zi(j)
        f1z_got(zz)
        f1y(y, zz, 2, y2)
        f1y_start(zz)
    f2z_got(zi(-2 * turn))
    f2z(zi(-2 * turn), 4, zi(2 * turn))
    f2z(zi(-2 * turn), 5, zi(turn))
    f2z_got(zi(2 * turn))
    f2z(zi(2 * turn), 6, zi(-turn))
    f1y_forward(zi(3))
    f1y_forward(zi(5))

    own[2].wait()
    own[3].wait()
    cots.finish()
    for j in range(1, NT):
        k = ti(j)
        arrived(pb.at[k], pxs.at[0], pxr.at[k])

    def part(i, _):
        k0, k1 = lax.div(i, 4), lax.rem(i, 4)
        at = pl.ds(pl.multiple_of(k0 * 256, 256), 256)
        cols = pl.ds(pl.multiple_of(k1 * 128, 128), 128)
        v = jnp.zeros((256, 128), F32)
        for k in range(NT):
            v = v + lax.dot_general(
                cf[k, at, :], pb[k, cols, :], (((1,), (1,)), ((), ())), preferred_element_type=F32
            )
        igrad[at, cols] = v.astype(BF16)
        return 0

    lax.fori_loop(0, 8, part, 0)

    for j in (2, 6):
        f1y_got(yb, zi(j))
        show(yb, zi(j), False)
    for k in range(NY):
        show(k, z, True)
    for j in (2, 6):
        for k in range(NY):
            show(k, zi(j), True)
    for j in (0, 1, 7, 4, 3, 5, 2, 6):
        zz = zi(j)
        f1y_got(yf, zz)
        show(yf, zz, False)
        f1y_got(y2, zz)
        show(y2, zz, False)
        if j in (1, 7, 3, 5, 4):
            f2z_got(zz)
            for k in range(NY):
                show(k, zz, True)
    for d in sent:
        d.wait_send()


def on_device(attention, cotangent, projection):
    dma = pltpu.SemaphoreType.DMA

    def hbm(a):
        return pltpu.with_memory_space_constraint(a, pltpu.HBM)

    v = pltpu.VMEM
    igrad, comb = pl.pallas_call(
        body,
        out_shape=(
            jax.ShapeDtypeStruct((512, 512), BF16),
            jax.ShapeDtypeStruct((NY, NZ, 128, 256), F32),
        ),
        in_specs=[pl.BlockSpec(memory_space=pl.ANY)] * 3,
        out_specs=(
            pl.BlockSpec(memory_space=pltpu.VMEM),
            pl.BlockSpec(memory_space=pltpu.VMEM),
        ),
        scratch_shapes=[
            v((H, NT, 16, 512), BF16),
            v((H, NT, NY, 2, 16, 512), BF16),
            v((NY, 512, 256), BF16),
            v((NT, 512, 256), BF16),
            v((NT, 512, 256), BF16),
            v((NY, NZ, 256, 128), F32),
            v((NZ, 256, 128), F32),
            v((NZ, 256, 128), F32),
            v((NZ, 272, 128), BF16),
            v((NZ, 272, 128), BF16),
            v((NY, NZ, 128, 256), BF16),
            v((128, 256), F32),
            v((128, 128), F32),
            v((NY * NT, 8, 128), F32),
            v((NT, 8, 128), F32),
            v((NY * NZ, 8, 128), F32),
            dma((8,)),
            dma((H, NT)),
            dma((H, NT)),
            dma((H, NY)),
            dma((H, NY)),
            dma((H, 7)),
            dma((H, NT)),
            dma((3,)),
            dma((NY,)),
            dma((7,)),
            dma((NT,)),
            dma((NT,)),
            dma((NT,)),
            dma((NY * NT,)),
            dma((NY * NT,)),
            dma((NZ,)),
            dma((NZ,)),
            dma((NT,)),
            dma((NT,)),
            dma((NY * NZ,)),
            dma((NY * NZ,)),
            dma((NZ,)),
            dma((NZ,)),
            dma((3, NZ)),
            dma((NY, NZ)),
            dma((NY,)),
            dma((NY,)),
            dma((7,)),
            dma((NZ,)),
        ],
        compiler_params=pltpu.CompilerParams(
            collective_id=0, has_side_effects=True, vmem_limit_bytes=48 * 1024 * 1024
        ),
        cost_estimate=pl.CostEstimate(
            flops=4 * 2**30, bytes_accessed=16 * 2**20, transcendentals=0
        ),
    )(
        hbm(attention.reshape(H, NT, 16, 512)),
        hbm(cotangent),
        hbm(projection.reshape(NT, 512, 256)),
    )
    return (igrad, comb.reshape(4096, 256))


def solution(mesh):
    return jax.shard_map(
        on_device,
        mesh=mesh,
        in_specs=(P("dp", "tensor"), P("dp", "tensor"), P(None, "tensor")),
        out_specs=(P("dp", "tensor"), P(None, "tensor")),
        check_vma=False,
    )
```

```python
import math

import jax
import jax.numpy as jnp
from jax import lax
from jax.experimental import pallas as pl
from jax.experimental.pallas import tpu as pltpu
from jax.sharding import PartitionSpec as P

EPS = 1e-06
MESH = pl.DeviceIdType.MESH
NX, NC, NY, NZ = 4, 2, 4, 8
NT = NX * NC
F32 = jnp.float32
BF16 = jnp.bfloat16
CUT = 112


MU_Z = 2.0**8 - 1
MU_F = 2.0**12 - 1
TOP = 125.0
H = 4


def encode(v, inv, mu):
    k = jnp.log(1.0 + jnp.abs(v) * (inv * mu)) * (2 * TOP / math.log(1.0 + mu)) - TOP
    e = jnp.exp2(k)
    return jnp.where(v < 0, -e, e).astype(BF16)


def decode(q, scale, mu):
    q = q.astype(F32)
    a = math.log(1.0 + mu) / (2 * TOP)
    h = jnp.log(jnp.abs(q)) * (a / math.log(2.0)) + TOP * a
    u = (jnp.exp(h) - 1.0) * (scale * (1.0 / mu))
    return jnp.where(q < 0, -u, u)


def pairs(n):
    return [(i, j) for i in range(n) for j in range(i, n)]


def tree_weights(rows, n):
    table = {}
    for k, (i, j) in enumerate(pairs(n)):
        table[i, j] = table[j, i] = rows[k]
    weights = [None] * n
    span, m = 1, n
    while m > 1:
        half = m // 2
        coef = []
        for i in range(half):
            aa = jnp.maximum(table[2 * i, 2 * i], 0.0)
            bb = jnp.maximum(table[2 * i + 1, 2 * i + 1], 0.0)
            s = table[2 * i, 2 * i + 1]
            coef.append(1.0 - s / (2.0 * (aa + EPS)))
            coef.append(1.0 - s / (2.0 * (bb + EPS)))
        for k in range(n):
            c = coef[k // span]
            weights[k] = c if weights[k] is None else weights[k] * c
        if half > 1:
            new = {}
            for i in range(half):
                for j in range(i, half):
                    if i == j:
                        a, b = 2 * i, 2 * i + 1
                        v = (
                            coef[a] * coef[a] * table[a, a]
                            + coef[b] * coef[b] * table[b, b]
                            + 2.0 * (coef[a] * coef[b] * table[a, b])
                        )
                    else:
                        v = coef[2 * i] * (
                            coef[2 * j] * table[2 * i, 2 * j]
                            + coef[2 * j + 1] * table[2 * i, 2 * j + 1]
                        ) + coef[2 * i + 1] * (
                            coef[2 * j] * table[2 * i + 1, 2 * j]
                            + coef[2 * j + 1] * table[2 * i + 1, 2 * j + 1]
                        )
                    new[i, j] = new[j, i] = v
            table = new
        span, m = span * 2, half
    return weights


def body(
    att,
    cot,
    proj,
    igrad,
    fin,
    s1,
    ab,
    cb,
    cf,
    pb,
    g,
    mz,
    rz,
    qz,
    rq,
    fc,
    mt,
    st,
    sr,
    tr1,
    tr2,
    loc,
    a1s,
    a1r,
    b1s,
    b1r,
    c1s,
    c1r,
    cys,
    cyr,
    cfs,
    cfr,
    pxs,
    pxr,
    g1s,
    g1r,
    zs,
    zr,
    h1s,
    h1r,
    h2s,
    h2r,
    f1zs,
    f1zr,
    f1ys,
    f1yr,
    f2ys,
    f2yr,
    f2zs,
    f2zr,
):
    dp = lax.axis_index("dp")
    t = lax.axis_index("tensor")
    z, y = lax.div(dp, NY), lax.rem(dp, NY)
    x, c = lax.div(t, NC), lax.rem(t, NC)
    turn = 1 - 2 * c
    sib = 1 - c

    def xi(d):
        return lax.rem(x + d + NX, NX)

    def yi(d):
        return lax.rem(y + d + NY, NY)

    def zi(d):
        return lax.rem(z + d + NZ, NZ)

    def dev(z_=None, y_=None, t_=None):
        z_ = z if z_ is None else z_
        y_ = y if y_ is None else y_
        t_ = t if t_ is None else t_
        return {"dp": z_ * NY + y_, "tensor": t_}

    def copy(src, dst, ss, rs, to):
        return pltpu.make_async_remote_copy(
            src_ref=src, dst_ref=dst, send_sem=ss, recv_sem=rs, device_id=to, device_id_type=MESH
        )

    sent = []

    def send(src, dst, ss, rs, to):
        d = copy(src, dst, ss, rs, to)
        d.start()
        sent.append(d)

    def arrived(ref, ss, rs):
        copy(ref, ref, ss, rs, dev()).wait_recv()

    barrier = pltpu.get_barrier_semaphore()
    for j in range(1, NT):
        pl.semaphore_signal(barrier, 1, device_id=dev(t_=lax.rem(t + j, NT)), device_id_type=MESH)
    for j in range(1, NY):
        pl.semaphore_signal(barrier, 1, device_id=dev(y_=yi(j)), device_id_type=MESH)
    for j in range(1, NZ):
        pl.semaphore_signal(barrier, 1, device_id=dev(z_=zi(j)), device_id_type=MESH)
    own = [
        pltpu.make_async_copy(att.at[:, t], s1.at[:, t], loc.at[0]),
        pltpu.make_async_copy(cot, cb.at[y], loc.at[1]),
        pltpu.make_async_copy(cot, cf.at[t], loc.at[2]),
        pltpu.make_async_copy(proj.at[t], pb.at[t], loc.at[3]),
    ]
    for d in own:
        d.start()
    st[...] = jnp.zeros_like(st)
    pl.semaphore_wait(barrier, (NT - 1) + (NY - 1) + (NZ - 1))

    def ti(j):
        return lax.rem(t + j, NT)

    yb, yf, y2 = yi(-turn), yi(turn), yi(2)

    class RowGather:
        def __init__(self, buf, ss, rs, first):
            self.buf, self.ss, self.rs = buf, ss, rs
            self.put(first, t, 0, NC * xi(1) + c)
            self.put(first, t, 1, NC * xi(-1) + c)
            self.put(first, t, 2, NC * x + sib)

        def put(self, src, slot, k, to):
            send(src, self.buf.at[slot], self.ss.at[k], self.rs.at[slot], dev(t_=to))

        def got(self, slot):
            arrived(self.buf.at[slot], self.ss.at[0], self.rs.at[slot])

        def forward(self):
            xb, xf = NC * xi(-turn) + c, NC * xi(turn) + c
            self.got(xb)
            self.put(self.buf.at[xb], xb, 3, xf)
            self.put(self.buf.at[xb], xb, 4, NC * x + sib)
            self.got(xf)
            self.put(self.buf.at[xf], xf, 5, NC * x + sib)

        def last(self):
            x2 = NC * xi(2) + c
            self.got(x2)
            self.put(self.buf.at[x2], x2, 6, NC * x + sib)

        def finish(self):
            for j in range(NX):
                self.got(NC * xi(j) + sib)

    for h in range(H):
        for j in (4, 5, 3, 2, 6, 1, 7):
            to = ti(j)
            send(att.at[h, to], s1.at[h, t], a1s.at[h, j], a1r.at[h, t], dev(t_=to))
    mine = []
    own[0].wait()
    for h in range(H):
        for j in range(1, NT):
            s = ti(j)
            arrived(s1.at[h, s], a1s.at[h, 0], a1r.at[h, s])
        for j in (2, 1, 3):
            q = yi(j)
            send(s1.at[h, pl.ds(2 * q, 2)], ab.at[h, t, y], b1s.at[h, j], b1r.at[h, y], dev(y_=q))
        mine.append(
            pltpu.make_async_copy(s1.at[h, pl.ds(2 * y, 2)], ab.at[h, t, y], loc.at[4 + h])
        )
        mine[h].start()
    send(cot, cb.at[y], cys.at[0], cyr.at[y], dev(y_=yi(1)))
    send(cot, cb.at[y], cys.at[1], cyr.at[y], dev(y_=yi(-1)))

    def row_ready(h):
        for j in range(1, NY):
            q = yi(j)
            arrived(ab.at[h, t, q], b1s.at[h, 0], b1r.at[h, q])
        mine[h].wait()
        return RowGather(ab.at[h], c1s.at[h], c1r.at[h], ab.at[h, t])

    rows = [row_ready(0), row_ready(1)]
    rows.append(row_ready(2))
    rows[0].forward()
    rows.append(row_ready(3))
    rows[1].forward()
    arrived(cb.at[yb], cys.at[0], cyr.at[yb])
    send(cb.at[yb], cb.at[yb], cys.at[2], cyr.at[yb], dev(y_=yf))
    rows[0].last()
    rows[2].forward()
    rows[1].last()
    rows[3].forward()
    rows[2].last()
    rows[0].finish()
    rows[1].finish()

    def grad(h):
        def one(i, _):
            r, b = lax.div(i, 2), lax.rem(i, 2)
            a = ab[2 * h : 2 * h + 2, :, r, b].reshape(256, 512)
            v = lax.dot_general(
                cb[r, 256 * h : 256 * (h + 1), :],
                a,
                (((0,), (0,)), ((), ())),
                preferred_element_type=F32,
            )
            for k in range(4):
                u = v[:, 128 * k : 128 * (k + 1)]
                g[r, 4 * b + k] = u if h == 0 else g[r, 4 * b + k] + u
            return 0

        lax.fori_loop(0, 8, one, 0)

    own[1].wait()
    arrived(cb.at[yf], cys.at[0], cyr.at[yf])
    arrived(cb.at[y2], cys.at[0], cyr.at[y2])
    grad(0)
    rows[3].last()
    rows[2].finish()
    rows[3].finish()
    grad(1)

    def dots(load, n, steps, top):
        pn = pairs(n)

        def one(i, acc):
            v = [load(k, i) for k in range(n)]
            new = [a + v[p] * v[q] for a, (p, q) in zip(acc, pn)]
            if top:
                new += [jnp.maximum(a, jnp.abs(u)) for a, u in zip(acc[len(pn) :], v)]
            return tuple(new)

        size = len(pn) + (n if top else 0)
        acc = lax.fori_loop(
            0, steps, one, tuple(jnp.zeros((8, 128), F32) for _ in range(size)), unroll=2
        )
        for k, a in enumerate(acc[: len(pn)]):
            st[k : k + 1, :] = jnp.sum(a, axis=0, keepdims=True)
        for k, a in enumerate(acc[len(pn) :]):
            m = jnp.max(jnp.max(a, axis=0, keepdims=True), axis=1, keepdims=True)
            st[len(pn) + k : len(pn) + k + 1, :] = jnp.broadcast_to(m * (1.0 / 128), (1, 128))
        row = jnp.sum(jnp.transpose(st[...]), axis=0, keepdims=True)
        return jnp.broadcast_to(row, (8, 128))

    def load_g(k, i):
        return g[k, lax.div(i, 32), pl.ds(pl.multiple_of(lax.rem(i, 32) * 8, 8), 8), :]

    local = dots(load_g, NY, 256, False)

    lane = lax.broadcasted_iota(jnp.int32, (8, 128), 1)
    maxima = lane >= len(pairs(NZ))

    def share(buf, slot, ss, rs, count, index, where, meanwhile=None):
        for j in range(1, count):
            send(buf.at[slot], buf.at[slot], ss.at[j], rs.at[slot], where(index(j)))
        if meanwhile is not None:
            meanwhile()
        for j in range(1, count):
            k = index(j)
            arrived(buf.at[k], ss.at[0], rs.at[k])
        total = top = buf[0]
        for k in range(1, count):
            total = total + buf[k]
            top = jnp.maximum(top, buf[k])
        return jnp.where(maxima, top, total)

    def spread(total, n):
        return [jnp.broadcast_to(total[0:1, k : k + 1], (1, 128)) for k in range(n)]

    def plane(j):
        return lax.rem(y * NT + t + j, NY * NT)

    me = y * NT + t
    sr[me] = local
    total = share(
        sr,
        me,
        g1s,
        g1r,
        NY * NT,
        plane,
        lambda k: dev(y_=lax.div(k, NT), t_=lax.rem(k, NT)),
    )
    cots = RowGather(cf, cfs, cfr, cot)
    w = tree_weights(spread(total, 10), NY)

    def merge_into(dst, load, ws):
        def one(i, top):
            at = pl.ds(pl.multiple_of(i * 8, 8), 8)
            v = load(0, at) * ws[0]
            for k in range(1, len(ws)):
                v = v + load(k, at) * ws[k]
            dst[at, :] = v
            return jnp.maximum(top, jnp.abs(v))

        top = lax.fori_loop(0, 32, one, jnp.zeros((8, 128), F32), unroll=2)
        return jnp.max(jnp.max(top, axis=0, keepdims=True), axis=1, keepdims=True)

    for j in (4, 3, 5, 2, 6, 1, 7, 0):
        zz = zi(j)
        top = merge_into(
            rz.at[z] if j == 0 else mz.at[zz], lambda k, at, zz=zz: g[k, zz, at, :], w
        )
        if j:
            scale = jnp.broadcast_to(jnp.maximum(top, 1e-30), (16, 128)).astype(BF16)
            qz[zz, 256:272, :] = scale
            inv = 1.0 / scale[0:1, :].astype(F32)

            def code(i, _, zz=zz, inv=inv):
                at = pl.ds(pl.multiple_of(i * 16, 16), 16)
                qz[zz, at, :] = encode(mz[zz, at, :], inv, MU_Z)
                return 0

            lax.fori_loop(0, 16, code, 0, unroll=2)
            send(qz.at[zz], rq.at[z], zs.at[j], zr.at[z], dev(z_=zz))

    cots.forward()
    for j in (1, 7, 2, 6, 3, 5, 4):
        k = zi(j)
        arrived(rq.at[k], zs.at[0], zr.at[k])
        scale = rq[k, 256:272, :].astype(F32)

        def uncode(i, _, k=k, scale=scale):
            at = pl.ds(pl.multiple_of(i * 16, 16), 16)
            rz[k, at, :] = decode(rq[k, at, :], scale, MU_Z)
            return 0

        lax.fori_loop(0, 16, uncode, 0, unroll=2)

    def load_r(k, i):
        return rz[k, pl.ds(pl.multiple_of(i * 8, 8), 8), :]

    cots.last()
    tr1[t] = dots(load_r, NZ, 32, True)
    tr2[dp] = share(tr1, t, h1s, h1r, NT, ti, lambda k: dev(t_=k))
    for j in (4, 5, 3, 2, 6, 1, 7):
        to = ti(j)
        send(proj.at[to], pb.at[t], pxs.at[j], pxr.at[t], dev(t_=to))
    total = share(
        tr2,
        dp,
        h2s,
        h2r,
        NY * NZ,
        lambda j: lax.rem(dp + j, NY * NZ),
        lambda k: {"dp": k, "tensor": t},
    )
    rows = spread(total, 44)
    w = tree_weights(rows, NZ)
    merge_into(mz.at[z], lambda k, at: rz[k, at, :], w)
    scale = jnp.full((1, 128), 1e-30, F32)
    for k in range(NZ):
        scale = scale + jnp.abs(w[k]) * rows[36 + k]
    scale = scale[0:1, 0:1]
    inv = 1.0 / scale
    mt[...] = jnp.transpose(mz[z])

    def code(i, _):
        at = pl.ds(pl.multiple_of(i * 16, 16), 16)
        fc[y, z, at, :] = encode(mt[at, :], inv, MU_F)
        return 0

    lax.fori_loop(0, 8, code, 0, unroll=2)

    def show(yy, zz, low):
        def one(i, _):
            at = pl.ds(pl.multiple_of(i * 16, 16), 16)
            fin[yy, zz, at, :] = decode(fc[yy, zz, at, :], scale, MU_F)
            return 0

        lo, hi = (CUT // 16, 8) if low else (0, CUT // 16)
        lax.fori_loop(lo, hi, one, 0, unroll=2)

    upper, lower = pl.ds(0, CUT), pl.ds(CUT, 128 - CUT)

    def f1z_got(zz):
        arrived(fc.at[y, zz, upper], f1zs.at[0], f1zr.at[zz])

    def f1y(yy, zz, k, to):
        r = fc.at[yy, zz, upper]
        send(r, r, f1ys.at[k, zz], f1yr.at[yy, zz], dev(y_=to))

    def f1y_got(yy, zz):
        arrived(fc.at[yy, zz, upper], f1ys.at[0, 0], f1yr.at[yy, zz])

    def f1y_start(zz):
        f1y(y, zz, 0, yf)
        f1y(y, zz, 1, yb)
        show(y, zz, False)

    def f1y_forward(zz):
        f1y_got(yb, zz)
        f1y(yb, zz, 2, yf)
        show(yb, zz, False)

    def f2z(zz, k, to):
        r = fc.at[:, zz, lower]
        send(r, r, f2zs.at[k], f2zr.at[zz], dev(z_=to))

    def f2z_got(zz):
        arrived(fc.at[:, zz, lower], f2zs.at[0], f2zr.at[zz])

    r = fc.at[y, z, lower]
    for j in (2, 1, 3):
        send(r, r, f2ys.at[j], f2yr.at[y], dev(y_=yi(j)))
    r = fc.at[y, z, upper]
    for j in (1, 7, 4, 3, 5, 2, 6):
        send(r, r, f1zs.at[j], f1zr.at[z], dev(z_=zi(j)))
    f1y_start(z)
    for j in range(1, NY):
        k = yi(j)
        arrived(fc.at[k, z, lower], f2ys.at[0], f2yr.at[k])
    f2z(z, 0, zi(turn))
    f2z(z, 1, zi(-turn))
    f2z(z, 2, zi(2 * turn))
    f2z(z, 3, zi(-2 * turn))

    def start(*js):
        for j in js:
            f1z_got(zi(j))
            f1y_start(zi(j))

    start(1, 7)
    f1y_forward(z)
    start(4)
    f1y_forward(zi(1))
    f1y_forward(zi(7))
    start(3, 5)
    f1y_forward(zi(4))
    for j in (2, 6):
        zz = zi(j)
        f1z_got(zz)
        f1y(y, zz, 2, y2)
        f1y_start(zz)
    f2z_got(zi(-2 * turn))
    f2z(zi(-2 * turn), 4, zi(2 * turn))
    f2z(zi(-2 * turn), 5, zi(turn))
    f2z_got(zi(2 * turn))
    f2z(zi(2 * turn), 6, zi(-turn))
    f1y_forward(zi(3))
    f1y_forward(zi(5))

    own[2].wait()
    own[3].wait()
    cots.finish()
    for j in range(1, NT):
        k = ti(j)
        arrived(pb.at[k], pxs.at[0], pxr.at[k])

    def part(i, _):
        k0, k1 = lax.div(i, 4), lax.rem(i, 4)
        at = pl.ds(pl.multiple_of(k0 * 256, 256), 256)
        cols = pl.ds(pl.multiple_of(k1 * 128, 128), 128)
        v = jnp.zeros((256, 128), F32)
        for k in range(NT):
            v = v + lax.dot_general(
                cf[k, at, :], pb[k, cols, :], (((1,), (1,)), ((), ())), preferred_element_type=F32
            )
        igrad[at, cols] = v.astype(BF16)
        return 0

    lax.fori_loop(0, 8, part, 0)

    for j in (2, 6):
        f1y_got(yb, zi(j))
        show(yb, zi(j), False)
    for k in range(NY):
        show(k, z, True)
    for j in (2, 6):
        for k in range(NY):
            show(k, zi(j), True)
    for j in (0, 1, 7, 4, 3, 5, 2, 6):
        zz = zi(j)
        f1y_got(yf, zz)
        show(yf, zz, False)
        f1y_got(y2, zz)
        show(y2, zz, False)
        if j in (1, 7, 3, 5, 4):
            f2z_got(zz)
            for k in range(NY):
                show(k, zz, True)
    for d in sent:
        d.wait_send()


def leave(igrad, comb, igrad_out, comb_out, sem):
    copies = [
        pltpu.make_async_copy(
            comb.at[1024 * k : 1024 * (k + 1)], comb_out.at[1024 * k : 1024 * (k + 1)], sem.at[k]
        )
        for k in range(4)
    ]
    copies.append(pltpu.make_async_copy(igrad, igrad_out, sem.at[4]))
    for d in copies:
        d.start()
    for d in copies:
        d.wait()


def on_device(attention, cotangent, projection):
    dma = pltpu.SemaphoreType.DMA

    def hbm(a):
        return pltpu.with_memory_space_constraint(a, pltpu.HBM)

    v = pltpu.VMEM
    igrad, comb = pl.pallas_call(
        body,
        out_shape=(
            jax.ShapeDtypeStruct((512, 512), BF16),
            jax.ShapeDtypeStruct((NY, NZ, 128, 256), F32),
        ),
        in_specs=[pl.BlockSpec(memory_space=pl.ANY)] * 3,
        out_specs=(
            pl.BlockSpec(memory_space=pltpu.VMEM),
            pl.BlockSpec(memory_space=pltpu.VMEM),
        ),
        scratch_shapes=[
            v((H, NT, 16, 512), BF16),
            v((H, NT, NY, 2, 16, 512), BF16),
            v((NY, 512, 256), BF16),
            v((NT, 512, 256), BF16),
            v((NT, 512, 256), BF16),
            v((NY, NZ, 256, 128), F32),
            v((NZ, 256, 128), F32),
            v((NZ, 256, 128), F32),
            v((NZ, 272, 128), BF16),
            v((NZ, 272, 128), BF16),
            v((NY, NZ, 128, 256), BF16),
            v((128, 256), F32),
            v((128, 128), F32),
            v((NY * NT, 8, 128), F32),
            v((NT, 8, 128), F32),
            v((NY * NZ, 8, 128), F32),
            dma((8,)),
            dma((H, NT)),
            dma((H, NT)),
            dma((H, NY)),
            dma((H, NY)),
            dma((H, 7)),
            dma((H, NT)),
            dma((3,)),
            dma((NY,)),
            dma((7,)),
            dma((NT,)),
            dma((NT,)),
            dma((NT,)),
            dma((NY * NT,)),
            dma((NY * NT,)),
            dma((NZ,)),
            dma((NZ,)),
            dma((NT,)),
            dma((NT,)),
            dma((NY * NZ,)),
            dma((NY * NZ,)),
            dma((NZ,)),
            dma((NZ,)),
            dma((3, NZ)),
            dma((NY, NZ)),
            dma((NY,)),
            dma((NY,)),
            dma((7,)),
            dma((NZ,)),
        ],
        compiler_params=pltpu.CompilerParams(
            collective_id=0, has_side_effects=True, vmem_limit_bytes=48 * 1024 * 1024
        ),
        cost_estimate=pl.CostEstimate(
            flops=4 * 2**30, bytes_accessed=16 * 2**20, transcendentals=0
        ),
    )(
        hbm(attention.reshape(H, NT, 16, 512)),
        hbm(cotangent),
        hbm(projection.reshape(NT, 512, 256)),
    )
    return pl.pallas_call(
        leave,
        out_shape=(
            jax.ShapeDtypeStruct((512, 512), BF16),
            jax.ShapeDtypeStruct((4096, 256), F32),
        ),
        in_specs=[pl.BlockSpec(memory_space=pltpu.VMEM)] * 2,
        out_specs=[pl.BlockSpec(memory_space=pltpu.HBM)] * 2,
        scratch_shapes=[dma((5,))],
        compiler_params=pltpu.CompilerParams(vmem_limit_bytes=1024 * 1024),
        cost_estimate=pl.CostEstimate(flops=0, bytes_accessed=9 * 2**20, transcendentals=0),
    )(
        pltpu.with_memory_space_constraint(igrad, pltpu.VMEM),
        pltpu.with_memory_space_constraint(comb.reshape(4096, 256), pltpu.VMEM),
    )


def solution(mesh):
    return jax.shard_map(
        on_device,
        mesh=mesh,
        in_specs=(P("dp", "tensor"), P("dp", "tensor"), P(None, "tensor")),
        out_specs=(P("dp", "tensor"), P(None, "tensor")),
        check_vma=False,
    )
```

```python
import math

import jax
import jax.numpy as jnp
from jax import lax
from jax.experimental import pallas as pl
from jax.experimental.pallas import tpu as pltpu
from jax.sharding import PartitionSpec as P

EPS = 1e-06
MESH = pl.DeviceIdType.MESH
NX, NC, NY, NZ = 4, 2, 4, 8
NT = NX * NC
F32 = jnp.float32
BF16 = jnp.bfloat16
CUT = 112


MU_Z = 2.0**8 - 1
MU_F = 2.0**12 - 1
TOP = 125.0
H = 4


def encode(v, inv, mu):
    k = jnp.log(1.0 + jnp.abs(v) * (inv * mu)) * (2 * TOP / math.log(1.0 + mu)) - TOP
    e = jnp.exp2(k)
    return jnp.where(v < 0, -e, e).astype(BF16)


def decode(q, scale, mu):
    q = q.astype(F32)
    a = math.log(1.0 + mu) / (2 * TOP)
    h = jnp.log(jnp.abs(q)) * (a / math.log(2.0)) + TOP * a
    u = (jnp.exp(h) - 1.0) * (scale * (1.0 / mu))
    return jnp.where(q < 0, -u, u)


def pairs(n):
    return [(i, j) for i in range(n) for j in range(i, n)]


def tree_weights(rows, n):
    table = {}
    for k, (i, j) in enumerate(pairs(n)):
        table[i, j] = table[j, i] = rows[k]
    weights = [None] * n
    span, m = 1, n
    while m > 1:
        half = m // 2
        coef = []
        for i in range(half):
            aa = jnp.maximum(table[2 * i, 2 * i], 0.0)
            bb = jnp.maximum(table[2 * i + 1, 2 * i + 1], 0.0)
            s = table[2 * i, 2 * i + 1]
            coef.append(1.0 - s / (2.0 * (aa + EPS)))
            coef.append(1.0 - s / (2.0 * (bb + EPS)))
        for k in range(n):
            c = coef[k // span]
            weights[k] = c if weights[k] is None else weights[k] * c
        if half > 1:
            new = {}
            for i in range(half):
                for j in range(i, half):
                    if i == j:
                        a, b = 2 * i, 2 * i + 1
                        v = (
                            coef[a] * coef[a] * table[a, a]
                            + coef[b] * coef[b] * table[b, b]
                            + 2.0 * (coef[a] * coef[b] * table[a, b])
                        )
                    else:
                        v = coef[2 * i] * (
                            coef[2 * j] * table[2 * i, 2 * j]
                            + coef[2 * j + 1] * table[2 * i, 2 * j + 1]
                        ) + coef[2 * i + 1] * (
                            coef[2 * j] * table[2 * i + 1, 2 * j]
                            + coef[2 * j + 1] * table[2 * i + 1, 2 * j + 1]
                        )
                    new[i, j] = new[j, i] = v
            table = new
        span, m = span * 2, half
    return weights


def body(
    att,
    cot,
    proj,
    igrad,
    fin,
    s1,
    ab,
    cb,
    cf,
    pb,
    g,
    mz,
    rz,
    qz,
    rq,
    fc,
    mt,
    st,
    sr,
    tr1,
    tr2,
    loc,
    a1s,
    a1r,
    b1s,
    b1r,
    c1s,
    c1r,
    cys,
    cyr,
    cfs,
    cfr,
    pxs,
    pxr,
    g1s,
    g1r,
    zs,
    zr,
    h1s,
    h1r,
    h2s,
    h2r,
    f1zs,
    f1zr,
    f1ys,
    f1yr,
    f2ys,
    f2yr,
    f2zs,
    f2zr,
):
    dp = lax.axis_index("dp")
    t = lax.axis_index("tensor")
    z, y = lax.div(dp, NY), lax.rem(dp, NY)
    x, c = lax.div(t, NC), lax.rem(t, NC)
    turn = 1 - 2 * c
    sib = 1 - c

    def xi(d):
        return lax.rem(x + d + NX, NX)

    def yi(d):
        return lax.rem(y + d + NY, NY)

    def zi(d):
        return lax.rem(z + d + NZ, NZ)

    def dev(z_=None, y_=None, t_=None):
        z_ = z if z_ is None else z_
        y_ = y if y_ is None else y_
        t_ = t if t_ is None else t_
        return {"dp": z_ * NY + y_, "tensor": t_}

    def copy(src, dst, ss, rs, to):
        return pltpu.make_async_remote_copy(
            src_ref=src, dst_ref=dst, send_sem=ss, recv_sem=rs, device_id=to, device_id_type=MESH
        )

    sent = []

    def send(src, dst, ss, rs, to):
        d = copy(src, dst, ss, rs, to)
        d.start()
        sent.append(d)

    def arrived(ref, ss, rs):
        copy(ref, ref, ss, rs, dev()).wait_recv()

    barrier = pltpu.get_barrier_semaphore()
    for j in range(1, NT):
        pl.semaphore_signal(barrier, 1, device_id=dev(t_=lax.rem(t + j, NT)), device_id_type=MESH)
    for j in range(1, NY):
        pl.semaphore_signal(barrier, 1, device_id=dev(y_=yi(j)), device_id_type=MESH)
    for j in range(1, NZ):
        pl.semaphore_signal(barrier, 1, device_id=dev(z_=zi(j)), device_id_type=MESH)
    own = [
        pltpu.make_async_copy(att.at[:, t], s1.at[:, t], loc.at[0]),
        pltpu.make_async_copy(cot, cb.at[y], loc.at[1]),
        pltpu.make_async_copy(cot, cf.at[t], loc.at[2]),
        pltpu.make_async_copy(proj.at[t], pb.at[t], loc.at[3]),
    ]
    for d in own:
        d.start()
    st[...] = jnp.zeros_like(st)
    pl.semaphore_wait(barrier, (NT - 1) + (NY - 1) + (NZ - 1))

    def ti(j):
        return lax.rem(t + j, NT)

    yb, yf, y2 = yi(-turn), yi(turn), yi(2)

    class RowGather:
        def __init__(self, buf, ss, rs, first):
            self.buf, self.ss, self.rs = buf, ss, rs
            self.put(first, t, 0, NC * xi(1) + c)
            self.put(first, t, 1, NC * xi(-1) + c)
            self.put(first, t, 2, NC * x + sib)

        def put(self, src, slot, k, to):
            send(src, self.buf.at[slot], self.ss.at[k], self.rs.at[slot], dev(t_=to))

        def got(self, slot):
            arrived(self.buf.at[slot], self.ss.at[0], self.rs.at[slot])

        def forward(self):
            xb, xf = NC * xi(-turn) + c, NC * xi(turn) + c
            self.got(xb)
            self.put(self.buf.at[xb], xb, 3, xf)
            self.put(self.buf.at[xb], xb, 4, NC * x + sib)
            self.got(xf)
            self.put(self.buf.at[xf], xf, 5, NC * x + sib)

        def last(self):
            x2 = NC * xi(2) + c
            self.got(x2)
            self.put(self.buf.at[x2], x2, 6, NC * x + sib)

        def finish(self):
            for j in range(NX):
                self.got(NC * xi(j) + sib)

    for h in range(H):
        for j in (4, 5, 3, 2, 6, 1, 7):
            to = ti(j)
            send(att.at[h, to], s1.at[h, t], a1s.at[h, j], a1r.at[h, t], dev(t_=to))
    mine = []
    own[0].wait()
    for h in range(H):
        for j in range(1, NT):
            s = ti(j)
            arrived(s1.at[h, s], a1s.at[h, 0], a1r.at[h, s])
        for j in (2, 1, 3):
            q = yi(j)
            send(s1.at[h, pl.ds(2 * q, 2)], ab.at[h, t, y], b1s.at[h, j], b1r.at[h, y], dev(y_=q))
        mine.append(
            pltpu.make_async_copy(s1.at[h, pl.ds(2 * y, 2)], ab.at[h, t, y], loc.at[4 + h])
        )
        mine[h].start()
    send(cot, cb.at[y], cys.at[0], cyr.at[y], dev(y_=yi(1)))
    send(cot, cb.at[y], cys.at[1], cyr.at[y], dev(y_=yi(-1)))

    def row_ready(h):
        for j in range(1, NY):
            q = yi(j)
            arrived(ab.at[h, t, q], b1s.at[h, 0], b1r.at[h, q])
        mine[h].wait()
        return RowGather(ab.at[h], c1s.at[h], c1r.at[h], ab.at[h, t])

    rows = [row_ready(0), row_ready(1)]
    rows.append(row_ready(2))
    rows[0].forward()
    rows.append(row_ready(3))
    rows[1].forward()
    arrived(cb.at[yb], cys.at[0], cyr.at[yb])
    send(cb.at[yb], cb.at[yb], cys.at[2], cyr.at[yb], dev(y_=yf))
    rows[0].last()
    rows[2].forward()
    rows[1].last()
    rows[3].forward()
    rows[2].last()
    rows[0].finish()
    rows[1].finish()

    def grad(h):
        def one(i, _):
            r, b = lax.div(i, 2), lax.rem(i, 2)
            a = ab[2 * h : 2 * h + 2, :, r, b].reshape(256, 512)
            v = lax.dot_general(
                cb[r, 256 * h : 256 * (h + 1), :],
                a,
                (((0,), (0,)), ((), ())),
                preferred_element_type=F32,
            )
            for k in range(4):
                u = v[:, 128 * k : 128 * (k + 1)]
                g[r, 4 * b + k] = u if h == 0 else g[r, 4 * b + k] + u
            return 0

        lax.fori_loop(0, 8, one, 0, unroll=4)

    own[1].wait()
    arrived(cb.at[yf], cys.at[0], cyr.at[yf])
    arrived(cb.at[y2], cys.at[0], cyr.at[y2])
    grad(0)
    rows[3].last()
    rows[2].finish()
    rows[3].finish()
    grad(1)

    def dots(load, n, steps, top):
        pn = pairs(n)

        def one(i, acc):
            v = [load(k, i) for k in range(n)]
            new = [a + v[p] * v[q] for a, (p, q) in zip(acc, pn)]
            if top:
                new += [jnp.maximum(a, jnp.abs(u)) for a, u in zip(acc[len(pn) :], v)]
            return tuple(new)

        size = len(pn) + (n if top else 0)
        acc = lax.fori_loop(
            0, steps, one, tuple(jnp.zeros((8, 128), F32) for _ in range(size)), unroll=8 if n == NY else 4
        )
        for k, a in enumerate(acc[: len(pn)]):
            st[k : k + 1, :] = jnp.sum(a, axis=0, keepdims=True)
        for k, a in enumerate(acc[len(pn) :]):
            m = jnp.max(jnp.max(a, axis=0, keepdims=True), axis=1, keepdims=True)
            st[len(pn) + k : len(pn) + k + 1, :] = jnp.broadcast_to(m * (1.0 / 128), (1, 128))
        row = jnp.sum(jnp.transpose(st[...]), axis=0, keepdims=True)
        return jnp.broadcast_to(row, (8, 128))

    def load_g(k, i):
        return g[k, lax.div(i, 32), pl.ds(pl.multiple_of(lax.rem(i, 32) * 8, 8), 8), :]

    local = dots(load_g, NY, 256, False)

    lane = lax.broadcasted_iota(jnp.int32, (8, 128), 1)
    maxima = lane >= len(pairs(NZ))

    def share(buf, slot, ss, rs, count, index, where, meanwhile=None):
        for j in range(1, count):
            send(buf.at[slot], buf.at[slot], ss.at[j], rs.at[slot], where(index(j)))
        if meanwhile is not None:
            meanwhile()
        for j in range(1, count):
            k = index(j)
            arrived(buf.at[k], ss.at[0], rs.at[k])
        total = top = buf[0]
        for k in range(1, count):
            total = total + buf[k]
            top = jnp.maximum(top, buf[k])
        return jnp.where(maxima, top, total)

    def spread(total, n):
        return [jnp.broadcast_to(total[0:1, k : k + 1], (1, 128)) for k in range(n)]

    def plane(j):
        return lax.rem(y * NT + t + j, NY * NT)

    me = y * NT + t
    sr[me] = local
    total = share(
        sr,
        me,
        g1s,
        g1r,
        NY * NT,
        plane,
        lambda k: dev(y_=lax.div(k, NT), t_=lax.rem(k, NT)),
    )
    cots = RowGather(cf, cfs, cfr, cot)
    w = tree_weights(spread(total, 10), NY)

    def merge_into(dst, load, ws):
        def one(i, top):
            at = pl.ds(pl.multiple_of(i * 8, 8), 8)
            v = load(0, at) * ws[0]
            for k in range(1, len(ws)):
                v = v + load(k, at) * ws[k]
            dst[at, :] = v
            return jnp.maximum(top, jnp.abs(v))

        top = lax.fori_loop(0, 32, one, jnp.zeros((8, 128), F32), unroll=8)
        return jnp.max(jnp.max(top, axis=0, keepdims=True), axis=1, keepdims=True)

    for j in (4, 3, 5, 2, 6, 1, 7, 0):
        zz = zi(j)
        top = merge_into(
            rz.at[z] if j == 0 else mz.at[zz], lambda k, at, zz=zz: g[k, zz, at, :], w
        )
        if j:
            scale = jnp.broadcast_to(jnp.maximum(top, 1e-30), (16, 128)).astype(BF16)
            qz[zz, 256:272, :] = scale
            inv = 1.0 / scale[0:1, :].astype(F32)

            def code(i, _, zz=zz, inv=inv):
                at = pl.ds(pl.multiple_of(i * 16, 16), 16)
                qz[zz, at, :] = encode(mz[zz, at, :], inv, MU_Z)
                return 0

            lax.fori_loop(0, 16, code, 0, unroll=8)
            send(qz.at[zz], rq.at[z], zs.at[j], zr.at[z], dev(z_=zz))

    cots.forward()
    for j in (1, 7, 2, 6, 3, 5, 4):
        k = zi(j)
        arrived(rq.at[k], zs.at[0], zr.at[k])
        scale = rq[k, 256:272, :].astype(F32)

        def uncode(i, _, k=k, scale=scale):
            at = pl.ds(pl.multiple_of(i * 16, 16), 16)
            rz[k, at, :] = decode(rq[k, at, :], scale, MU_Z)
            return 0

        lax.fori_loop(0, 16, uncode, 0, unroll=8)

    def load_r(k, i):
        return rz[k, pl.ds(pl.multiple_of(i * 8, 8), 8), :]

    cots.last()
    tr1[t] = dots(load_r, NZ, 32, True)
    tr2[dp] = share(tr1, t, h1s, h1r, NT, ti, lambda k: dev(t_=k))
    for j in (4, 5, 3, 2, 6, 1, 7):
        to = ti(j)
        send(proj.at[to], pb.at[t], pxs.at[j], pxr.at[t], dev(t_=to))
    total = share(
        tr2,
        dp,
        h2s,
        h2r,
        NY * NZ,
        lambda j: lax.rem(dp + j, NY * NZ),
        lambda k: {"dp": k, "tensor": t},
    )
    rows = spread(total, 44)
    w = tree_weights(rows, NZ)
    merge_into(mz.at[z], lambda k, at: rz[k, at, :], w)
    scale = jnp.full((1, 128), 1e-30, F32)
    for k in range(NZ):
        scale = scale + jnp.abs(w[k]) * rows[36 + k]
    scale = scale[0:1, 0:1]
    inv = 1.0 / scale
    mt[...] = jnp.transpose(mz[z])

    def code(i, _):
        at = pl.ds(pl.multiple_of(i * 16, 16), 16)
        fc[y, z, at, :] = encode(mt[at, :], inv, MU_F)
        return 0

    lax.fori_loop(0, 8, code, 0, unroll=8)

    def show(yy, zz, low):
        def one(i, _):
            at = pl.ds(pl.multiple_of(i * 16, 16), 16)
            fin[yy, zz, at, :] = decode(fc[yy, zz, at, :], scale, MU_F)
            return 0

        lo, hi = (CUT // 16, 8) if low else (0, CUT // 16)
        lax.fori_loop(lo, hi, one, 0, unroll=hi - lo)

    upper, lower = pl.ds(0, CUT), pl.ds(CUT, 128 - CUT)

    def f1z_got(zz):
        arrived(fc.at[y, zz, upper], f1zs.at[0], f1zr.at[zz])

    def f1y(yy, zz, k, to):
        r = fc.at[yy, zz, upper]
        send(r, r, f1ys.at[k, zz], f1yr.at[yy, zz], dev(y_=to))

    def f1y_got(yy, zz):
        arrived(fc.at[yy, zz, upper], f1ys.at[0, 0], f1yr.at[yy, zz])

    def f1y_start(zz):
        f1y(y, zz, 0, yf)
        f1y(y, zz, 1, yb)
        show(y, zz, False)

    def f1y_forward(zz):
        f1y_got(yb, zz)
        f1y(yb, zz, 2, yf)
        show(yb, zz, False)

    def f2z(zz, k, to):
        r = fc.at[:, zz, lower]
        send(r, r, f2zs.at[k], f2zr.at[zz], dev(z_=to))

    def f2z_got(zz):
        arrived(fc.at[:, zz, lower], f2zs.at[0], f2zr.at[zz])

    r = fc.at[y, z, lower]
    for j in (2, 1, 3):
        send(r, r, f2ys.at[j], f2yr.at[y], dev(y_=yi(j)))
    r = fc.at[y, z, upper]
    for j in (1, 7, 4, 3, 5, 2, 6):
        send(r, r, f1zs.at[j], f1zr.at[z], dev(z_=zi(j)))
    f1y_start(z)
    for j in range(1, NY):
        k = yi(j)
        arrived(fc.at[k, z, lower], f2ys.at[0], f2yr.at[k])
    f2z(z, 0, zi(turn))
    f2z(z, 1, zi(-turn))
    f2z(z, 2, zi(2 * turn))
    f2z(z, 3, zi(-2 * turn))

    def start(*js):
        for j in js:
            f1z_got(zi(j))
            f1y_start(zi(j))

    start(1, 7)
    f1y_forward(z)
    start(4)
    f1y_forward(zi(1))
    f1y_forward(zi(7))
    start(3, 5)
    f1y_forward(zi(4))
    for j in (2, 6):
        zz = zi(j)
        f1z_got(zz)
        f1y(y, zz, 2, y2)
        f1y_start(zz)
    f2z_got(zi(-2 * turn))
    f2z(zi(-2 * turn), 4, zi(2 * turn))
    f2z(zi(-2 * turn), 5, zi(turn))
    f2z_got(zi(2 * turn))
    f2z(zi(2 * turn), 6, zi(-turn))
    f1y_forward(zi(3))
    f1y_forward(zi(5))

    own[2].wait()
    own[3].wait()
    cots.finish()
    for j in range(1, NT):
        k = ti(j)
        arrived(pb.at[k], pxs.at[0], pxr.at[k])

    def part(i, _):
        k0, k1 = lax.div(i, 4), lax.rem(i, 4)
        at = pl.ds(pl.multiple_of(k0 * 256, 256), 256)
        cols = pl.ds(pl.multiple_of(k1 * 128, 128), 128)
        v = jnp.zeros((256, 128), F32)
        for k in range(NT):
            v = v + lax.dot_general(
                cf[k, at, :], pb[k, cols, :], (((1,), (1,)), ((), ())), preferred_element_type=F32
            )
        igrad[at, cols] = v.astype(BF16)
        return 0

    lax.fori_loop(0, 8, part, 0)

    for j in (2, 6):
        f1y_got(yb, zi(j))
        show(yb, zi(j), False)
    for k in range(NY):
        show(k, z, True)
    for j in (2, 6):
        for k in range(NY):
            show(k, zi(j), True)
    for j in (0, 1, 7, 4, 3, 5, 2, 6):
        zz = zi(j)
        f1y_got(yf, zz)
        show(yf, zz, False)
        f1y_got(y2, zz)
        show(y2, zz, False)
        if j in (1, 7, 3, 5, 4):
            f2z_got(zz)
            for k in range(NY):
                show(k, zz, True)
    for d in sent:
        d.wait_send()


def leave(igrad, comb, igrad_out, comb_out, sem):
    copies = [
        pltpu.make_async_copy(
            comb.at[1024 * k : 1024 * (k + 1)], comb_out.at[1024 * k : 1024 * (k + 1)], sem.at[k]
        )
        for k in range(4)
    ]
    copies.append(pltpu.make_async_copy(igrad, igrad_out, sem.at[4]))
    for d in copies:
        d.start()
    for d in copies:
        d.wait()


def on_device(attention, cotangent, projection):
    dma = pltpu.SemaphoreType.DMA

    def hbm(a):
        return pltpu.with_memory_space_constraint(a, pltpu.HBM)

    v = pltpu.VMEM
    igrad, comb = pl.pallas_call(
        body,
        out_shape=(
            jax.ShapeDtypeStruct((512, 512), BF16),
            jax.ShapeDtypeStruct((NY, NZ, 128, 256), F32),
        ),
        in_specs=[pl.BlockSpec(memory_space=pl.ANY)] * 3,
        out_specs=(
            pl.BlockSpec(memory_space=pltpu.VMEM),
            pl.BlockSpec(memory_space=pltpu.VMEM),
        ),
        scratch_shapes=[
            v((H, NT, 16, 512), BF16),
            v((H, NT, NY, 2, 16, 512), BF16),
            v((NY, 512, 256), BF16),
            v((NT, 512, 256), BF16),
            v((NT, 512, 256), BF16),
            v((NY, NZ, 256, 128), F32),
            v((NZ, 256, 128), F32),
            v((NZ, 256, 128), F32),
            v((NZ, 272, 128), BF16),
            v((NZ, 272, 128), BF16),
            v((NY, NZ, 128, 256), BF16),
            v((128, 256), F32),
            v((128, 128), F32),
            v((NY * NT, 8, 128), F32),
            v((NT, 8, 128), F32),
            v((NY * NZ, 8, 128), F32),
            dma((8,)),
            dma((H, NT)),
            dma((H, NT)),
            dma((H, NY)),
            dma((H, NY)),
            dma((H, 7)),
            dma((H, NT)),
            dma((3,)),
            dma((NY,)),
            dma((7,)),
            dma((NT,)),
            dma((NT,)),
            dma((NT,)),
            dma((NY * NT,)),
            dma((NY * NT,)),
            dma((NZ,)),
            dma((NZ,)),
            dma((NT,)),
            dma((NT,)),
            dma((NY * NZ,)),
            dma((NY * NZ,)),
            dma((NZ,)),
            dma((NZ,)),
            dma((3, NZ)),
            dma((NY, NZ)),
            dma((NY,)),
            dma((NY,)),
            dma((7,)),
            dma((NZ,)),
        ],
        compiler_params=pltpu.CompilerParams(
            collective_id=0, has_side_effects=True, vmem_limit_bytes=48 * 1024 * 1024
        ),
        cost_estimate=pl.CostEstimate(
            flops=4 * 2**30, bytes_accessed=16 * 2**20, transcendentals=0
        ),
    )(
        hbm(attention.reshape(H, NT, 16, 512)),
        hbm(cotangent),
        hbm(projection.reshape(NT, 512, 256)),
    )
    return pl.pallas_call(
        leave,
        out_shape=(
            jax.ShapeDtypeStruct((512, 512), BF16),
            jax.ShapeDtypeStruct((4096, 256), F32),
        ),
        in_specs=[pl.BlockSpec(memory_space=pltpu.VMEM)] * 2,
        out_specs=[pl.BlockSpec(memory_space=pltpu.HBM)] * 2,
        scratch_shapes=[dma((5,))],
        compiler_params=pltpu.CompilerParams(vmem_limit_bytes=1024 * 1024),
        cost_estimate=pl.CostEstimate(flops=0, bytes_accessed=9 * 2**20, transcendentals=0),
    )(
        pltpu.with_memory_space_constraint(igrad, pltpu.VMEM),
        pltpu.with_memory_space_constraint(comb.reshape(4096, 256), pltpu.VMEM),
    )


def solution(mesh):
    return jax.shard_map(
        on_device,
        mesh=mesh,
        in_specs=(P("dp", "tensor"), P("dp", "tensor"), P(None, "tensor")),
        out_specs=(P("dp", "tensor"), P(None, "tensor")),
        check_vma=False,
    )
```

```python
import math

import jax
import jax.numpy as jnp
from jax import lax
from jax.experimental import pallas as pl
from jax.experimental.pallas import tpu as pltpu
from jax.sharding import PartitionSpec as P

EPS = 1e-06
MESH = pl.DeviceIdType.MESH
NX, NC, NY, NZ = 4, 2, 4, 8
NT = NX * NC
F32 = jnp.float32
BF16 = jnp.bfloat16
CUT = 112


MU_Z = 2.0**8 - 1
MU_F = 2.0**12 - 1
TOP = 125.0
H = 4


def encode(v, inv, mu):
    k = jnp.log(1.0 + jnp.abs(v) * (inv * mu)) * (2 * TOP / math.log(1.0 + mu)) - TOP
    e = jnp.exp2(k)
    return jnp.where(v < 0, -e, e).astype(BF16)


def decode(q, scale, mu):
    q = q.astype(F32)
    a = math.log(1.0 + mu) / (2 * TOP)
    h = jnp.log(jnp.abs(q)) * (a / math.log(2.0)) + TOP * a
    u = (jnp.exp(h) - 1.0) * (scale * (1.0 / mu))
    return jnp.where(q < 0, -u, u)


def pairs(n):
    return [(i, j) for i in range(n) for j in range(i, n)]


def tree_weights(rows, n):
    table = {}
    for k, (i, j) in enumerate(pairs(n)):
        table[i, j] = table[j, i] = rows[k]
    weights = [None] * n
    span, m = 1, n
    while m > 1:
        half = m // 2
        coef = []
        for i in range(half):
            aa = jnp.maximum(table[2 * i, 2 * i], 0.0)
            bb = jnp.maximum(table[2 * i + 1, 2 * i + 1], 0.0)
            s = table[2 * i, 2 * i + 1]
            coef.append(1.0 - s / (2.0 * (aa + EPS)))
            coef.append(1.0 - s / (2.0 * (bb + EPS)))
        for k in range(n):
            c = coef[k // span]
            weights[k] = c if weights[k] is None else weights[k] * c
        if half > 1:
            new = {}
            for i in range(half):
                for j in range(i, half):
                    if i == j:
                        a, b = 2 * i, 2 * i + 1
                        v = (
                            coef[a] * coef[a] * table[a, a]
                            + coef[b] * coef[b] * table[b, b]
                            + 2.0 * (coef[a] * coef[b] * table[a, b])
                        )
                    else:
                        v = coef[2 * i] * (
                            coef[2 * j] * table[2 * i, 2 * j]
                            + coef[2 * j + 1] * table[2 * i, 2 * j + 1]
                        ) + coef[2 * i + 1] * (
                            coef[2 * j] * table[2 * i + 1, 2 * j]
                            + coef[2 * j + 1] * table[2 * i + 1, 2 * j + 1]
                        )
                    new[i, j] = new[j, i] = v
            table = new
        span, m = span * 2, half
    return weights


def body(
    att,
    cot,
    proj,
    igrad,
    fin,
    s1,
    ab,
    cb,
    cf,
    pb,
    g,
    mz,
    rz,
    qz,
    rq,
    fc,
    mt,
    st,
    sr,
    tr1,
    tr2,
    loc,
    a1s,
    a1r,
    b1s,
    b1r,
    c1s,
    c1r,
    cys,
    cyr,
    cfs,
    cfr,
    pxs,
    pxr,
    g1s,
    g1r,
    zs,
    zr,
    h1s,
    h1r,
    h2s,
    h2r,
    f1zs,
    f1zr,
    f1ys,
    f1yr,
    f2ys,
    f2yr,
    f2zs,
    f2zr,
):
    dp = lax.axis_index("dp")
    t = lax.axis_index("tensor")
    z, y = lax.div(dp, NY), lax.rem(dp, NY)
    x, c = lax.div(t, NC), lax.rem(t, NC)
    turn = 1 - 2 * c
    sib = 1 - c

    def xi(d):
        return lax.rem(x + d + NX, NX)

    def yi(d):
        return lax.rem(y + d + NY, NY)

    def zi(d):
        return lax.rem(z + d + NZ, NZ)

    def dev(z_=None, y_=None, t_=None):
        z_ = z if z_ is None else z_
        y_ = y if y_ is None else y_
        t_ = t if t_ is None else t_
        return {"dp": z_ * NY + y_, "tensor": t_}

    def copy(src, dst, ss, rs, to):
        return pltpu.make_async_remote_copy(
            src_ref=src, dst_ref=dst, send_sem=ss, recv_sem=rs, device_id=to, device_id_type=MESH
        )

    sent = []

    def send(src, dst, ss, rs, to):
        d = copy(src, dst, ss, rs, to)
        d.start()
        sent.append(d)

    def arrived(ref, ss, rs):
        copy(ref, ref, ss, rs, dev()).wait_recv()

    barrier = pltpu.get_barrier_semaphore()
    for j in range(1, NT):
        pl.semaphore_signal(barrier, 1, device_id=dev(t_=lax.rem(t + j, NT)), device_id_type=MESH)
    for j in range(1, NY):
        pl.semaphore_signal(barrier, 1, device_id=dev(y_=yi(j)), device_id_type=MESH)
    for j in range(1, NZ):
        pl.semaphore_signal(barrier, 1, device_id=dev(z_=zi(j)), device_id_type=MESH)
    own = [
        pltpu.make_async_copy(att.at[:, t], s1.at[:, t], loc.at[0]),
        pltpu.make_async_copy(cot, cb.at[y], loc.at[1]),
        pltpu.make_async_copy(cot, cf.at[t], loc.at[2]),
        pltpu.make_async_copy(proj.at[t], pb.at[t], loc.at[3]),
    ]
    for d in own:
        d.start()
    st[...] = jnp.zeros_like(st)
    pl.semaphore_wait(barrier, (NT - 1) + (NY - 1) + (NZ - 1))

    def ti(j):
        return lax.rem(t + j, NT)

    yb, yf, y2 = yi(-turn), yi(turn), yi(2)

    class RowGather:
        def __init__(self, buf, ss, rs, first):
            self.buf, self.ss, self.rs = buf, ss, rs
            self.put(first, t, 0, NC * xi(1) + c)
            self.put(first, t, 1, NC * xi(-1) + c)
            self.put(first, t, 2, NC * x + sib)

        def put(self, src, slot, k, to):
            send(src, self.buf.at[slot], self.ss.at[k], self.rs.at[slot], dev(t_=to))

        def got(self, slot):
            arrived(self.buf.at[slot], self.ss.at[0], self.rs.at[slot])

        def forward(self):
            xb, xf = NC * xi(-turn) + c, NC * xi(turn) + c
            self.got(xb)
            self.put(self.buf.at[xb], xb, 3, xf)
            self.put(self.buf.at[xb], xb, 4, NC * x + sib)
            self.got(xf)
            self.put(self.buf.at[xf], xf, 5, NC * x + sib)

        def last(self):
            x2 = NC * xi(2) + c
            self.got(x2)
            self.put(self.buf.at[x2], x2, 6, NC * x + sib)

        def finish(self):
            for j in range(NX):
                self.got(NC * xi(j) + sib)

    for h in range(H):
        for j in (4, 5, 3, 2, 6, 1, 7):
            to = ti(j)
            send(att.at[h, to], s1.at[h, t], a1s.at[h, j], a1r.at[h, t], dev(t_=to))
    mine = []
    own[0].wait()
    for h in range(H):
        for j in range(1, NT):
            s = ti(j)
            arrived(s1.at[h, s], a1s.at[h, 0], a1r.at[h, s])
        for j in (2, 1, 3):
            q = yi(j)
            send(s1.at[h, pl.ds(2 * q, 2)], ab.at[h, t, y], b1s.at[h, j], b1r.at[h, y], dev(y_=q))
        mine.append(
            pltpu.make_async_copy(s1.at[h, pl.ds(2 * y, 2)], ab.at[h, t, y], loc.at[4 + h])
        )
        mine[h].start()
    send(cot, cb.at[y], cys.at[0], cyr.at[y], dev(y_=yi(1)))
    send(cot, cb.at[y], cys.at[1], cyr.at[y], dev(y_=yi(-1)))

    def row_ready(h):
        for j in range(1, NY):
            q = yi(j)
            arrived(ab.at[h, t, q], b1s.at[h, 0], b1r.at[h, q])
        mine[h].wait()
        return RowGather(ab.at[h], c1s.at[h], c1r.at[h], ab.at[h, t])

    rows = [row_ready(0), row_ready(1)]
    rows.append(row_ready(2))
    rows[0].forward()
    rows.append(row_ready(3))
    rows[1].forward()
    arrived(cb.at[yb], cys.at[0], cyr.at[yb])
    send(cb.at[yb], cb.at[yb], cys.at[2], cyr.at[yb], dev(y_=yf))
    rows[0].last()
    rows[2].forward()
    rows[1].last()
    rows[3].forward()
    rows[2].last()
    rows[0].finish()
    rows[1].finish()

    def grad(h):
        def one(i, _):
            r, b = lax.div(i, 2), lax.rem(i, 2)
            a = ab[2 * h : 2 * h + 2, :, r, b].reshape(256, 512)
            v = lax.dot_general(
                cb[r, 256 * h : 256 * (h + 1), :],
                a,
                (((0,), (0,)), ((), ())),
                preferred_element_type=F32,
            )
            for k in range(4):
                u = v[:, 128 * k : 128 * (k + 1)]
                g[r, 4 * b + k] = u if h == 0 else g[r, 4 * b + k] + u
            return 0

        lax.fori_loop(0, 8, one, 0, unroll=4)

    own[1].wait()
    arrived(cb.at[yf], cys.at[0], cyr.at[yf])
    arrived(cb.at[y2], cys.at[0], cyr.at[y2])
    grad(0)
    rows[3].last()
    rows[2].finish()
    rows[3].finish()
    grad(1)

    def dots(load, n, steps, top):
        pn = pairs(n)

        def one(i, acc):
            v = [load(k, i) for k in range(n)]
            new = [a + v[p] * v[q] for a, (p, q) in zip(acc, pn)]
            if top:
                new += [jnp.maximum(a, jnp.abs(u)) for a, u in zip(acc[len(pn) :], v)]
            return tuple(new)

        size = len(pn) + (n if top else 0)
        acc = lax.fori_loop(
            0, steps, one, tuple(jnp.zeros((8, 128), F32) for _ in range(size)), unroll=8 if n == NY else 4
        )
        for k, a in enumerate(acc[: len(pn)]):
            st[k : k + 1, :] = jnp.sum(a, axis=0, keepdims=True)
        for k, a in enumerate(acc[len(pn) :]):
            m = jnp.max(jnp.max(a, axis=0, keepdims=True), axis=1, keepdims=True)
            st[len(pn) + k : len(pn) + k + 1, :] = jnp.broadcast_to(m * (1.0 / 128), (1, 128))
        row = jnp.sum(jnp.transpose(st[...]), axis=0, keepdims=True)
        return jnp.broadcast_to(row, (8, 128))

    def load_g(k, i):
        return g[k, lax.div(i, 32), pl.ds(pl.multiple_of(lax.rem(i, 32) * 8, 8), 8), :]

    local = dots(load_g, NY, 256, False)

    lane = lax.broadcasted_iota(jnp.int32, (8, 128), 1)
    maxima = lane >= len(pairs(NZ))

    def share(buf, slot, ss, rs, count, index, where, meanwhile=None):
        for j in range(1, count):
            send(buf.at[slot], buf.at[slot], ss.at[j], rs.at[slot], where(index(j)))
        if meanwhile is not None:
            meanwhile()
        for j in range(1, count):
            k = index(j)
            arrived(buf.at[k], ss.at[0], rs.at[k])
        total = top = buf[0]
        for k in range(1, count):
            total = total + buf[k]
            top = jnp.maximum(top, buf[k])
        return jnp.where(maxima, top, total)

    def spread(total, n):
        return [jnp.broadcast_to(total[0:1, k : k + 1], (1, 128)) for k in range(n)]

    def plane(j):
        return lax.rem(y * NT + t + j, NY * NT)

    me = y * NT + t
    sr[me] = local
    total = share(
        sr,
        me,
        g1s,
        g1r,
        NY * NT,
        plane,
        lambda k: dev(y_=lax.div(k, NT), t_=lax.rem(k, NT)),
    )
    cots = RowGather(cf, cfs, cfr, cot)
    w = tree_weights(spread(total, 10), NY)

    def merge_into(dst, load, ws):
        def one(i, top):
            at = pl.ds(pl.multiple_of(i * 8, 8), 8)
            v = load(0, at) * ws[0]
            for k in range(1, len(ws)):
                v = v + load(k, at) * ws[k]
            dst[at, :] = v
            return jnp.maximum(top, jnp.abs(v))

        top = lax.fori_loop(0, 32, one, jnp.zeros((8, 128), F32), unroll=8)
        return jnp.max(jnp.max(top, axis=0, keepdims=True), axis=1, keepdims=True)

    for j in (4, 3, 5, 2, 6, 1, 7, 0):
        zz = zi(j)
        top = merge_into(
            rz.at[z] if j == 0 else mz.at[zz], lambda k, at, zz=zz: g[k, zz, at, :], w
        )
        if j:
            scale = jnp.broadcast_to(jnp.maximum(top, 1e-30), (16, 128)).astype(BF16)
            qz[zz, 256:272, :] = scale
            inv = 1.0 / scale[0:1, :].astype(F32)

            def code(i, _, zz=zz, inv=inv):
                at = pl.ds(pl.multiple_of(i * 16, 16), 16)
                qz[zz, at, :] = encode(mz[zz, at, :], inv, MU_Z)
                return 0

            lax.fori_loop(0, 16, code, 0, unroll=8)
            send(qz.at[zz], rq.at[z], zs.at[j], zr.at[z], dev(z_=zz))

    cots.forward()
    for j in (1, 7, 2, 6, 3, 5, 4):
        k = zi(j)
        arrived(rq.at[k], zs.at[0], zr.at[k])
        scale = rq[k, 256:272, :].astype(F32)

        def uncode(i, _, k=k, scale=scale):
            at = pl.ds(pl.multiple_of(i * 16, 16), 16)
            rz[k, at, :] = decode(rq[k, at, :], scale, MU_Z)
            return 0

        lax.fori_loop(0, 16, uncode, 0, unroll=8)

    def load_r(k, i):
        return rz[k, pl.ds(pl.multiple_of(i * 8, 8), 8), :]

    cots.last()
    tr1[t] = dots(load_r, NZ, 32, True)
    tr2[dp] = share(tr1, t, h1s, h1r, NT, ti, lambda k: dev(t_=k))
    for j in (4, 5, 3, 2, 6, 1, 7):
        to = ti(j)
        send(proj.at[to], pb.at[t], pxs.at[j], pxr.at[t], dev(t_=to))
    total = share(
        tr2,
        dp,
        h2s,
        h2r,
        NY * NZ,
        lambda j: lax.rem(dp + j, NY * NZ),
        lambda k: {"dp": k, "tensor": t},
    )
    rows = spread(total, 44)
    w = tree_weights(rows, NZ)
    merge_into(mz.at[z], lambda k, at: rz[k, at, :], w)
    scale = jnp.full((1, 128), 1e-30, F32)
    for k in range(NZ):
        scale = scale + jnp.abs(w[k]) * rows[36 + k]
    scale = scale[0:1, 0:1]
    inv = 1.0 / scale
    mt[...] = jnp.transpose(mz[z])

    def code(i, _):
        at = pl.ds(pl.multiple_of(i * 16, 16), 16)
        fc[y, z, at, :] = encode(mt[at, :], inv, MU_F)
        return 0

    lax.fori_loop(0, 8, code, 0, unroll=8)

    def show(yy, zz, low):
        def one(i, _):
            at = pl.ds(pl.multiple_of(i * 16, 16), 16)
            fin[yy, zz, at, :] = decode(fc[yy, zz, at, :], scale, MU_F)
            return 0

        lo, hi = (CUT // 16, 8) if low else (0, CUT // 16)
        lax.fori_loop(lo, hi, one, 0, unroll=hi - lo)

    upper, lower = pl.ds(0, CUT), pl.ds(CUT, 128 - CUT)

    def f1z_got(zz):
        arrived(fc.at[y, zz, upper], f1zs.at[0], f1zr.at[zz])

    def f1y(yy, zz, k, to):
        r = fc.at[yy, zz, upper]
        send(r, r, f1ys.at[k, zz], f1yr.at[yy, zz], dev(y_=to))

    def f1y_got(yy, zz):
        arrived(fc.at[yy, zz, upper], f1ys.at[0, 0], f1yr.at[yy, zz])

    def f1y_start(zz):
        f1y(y, zz, 0, yf)
        f1y(y, zz, 1, yb)
        show(y, zz, False)

    def f1y_forward(zz):
        f1y_got(yb, zz)
        f1y(yb, zz, 2, yf)
        show(yb, zz, False)

    def f2z(zz, k, to):
        r = fc.at[:, zz, lower]
        send(r, r, f2zs.at[k], f2zr.at[zz], dev(z_=to))

    def f2z_got(zz):
        arrived(fc.at[:, zz, lower], f2zs.at[0], f2zr.at[zz])

    r = fc.at[y, z, lower]
    for j in (2, 1, 3):
        send(r, r, f2ys.at[j], f2yr.at[y], dev(y_=yi(j)))
    r = fc.at[y, z, upper]
    for j in (1, 7, 4, 3, 5, 2, 6):
        send(r, r, f1zs.at[j], f1zr.at[z], dev(z_=zi(j)))
    f1y_start(z)
    for j in range(1, NY):
        k = yi(j)
        arrived(fc.at[k, z, lower], f2ys.at[0], f2yr.at[k])
    f2z(z, 0, zi(turn))
    f2z(z, 1, zi(-turn))
    f2z(z, 2, zi(2 * turn))
    f2z(z, 3, zi(-2 * turn))

    def start(*js):
        for j in js:
            f1z_got(zi(j))
            f1y_start(zi(j))

    start(1, 7)
    f1y_forward(z)
    start(4)
    f1y_forward(zi(1))
    f1y_forward(zi(7))
    start(3, 5)
    f1y_forward(zi(4))
    for j in (2, 6):
        zz = zi(j)
        f1z_got(zz)
        f1y(y, zz, 2, y2)
        f1y_start(zz)
    f2z_got(zi(-2 * turn))
    f2z(zi(-2 * turn), 4, zi(2 * turn))
    f2z(zi(-2 * turn), 5, zi(turn))
    f2z_got(zi(2 * turn))
    f2z(zi(2 * turn), 6, zi(-turn))
    f1y_forward(zi(3))
    f1y_forward(zi(5))

    own[2].wait()
    own[3].wait()
    cots.finish()
    for j in range(1, NT):
        k = ti(j)
        arrived(pb.at[k], pxs.at[0], pxr.at[k])

    def part(i, _):
        k0, k1 = lax.div(i, 4), lax.rem(i, 4)
        at = pl.ds(pl.multiple_of(k0 * 256, 256), 256)
        cols = pl.ds(pl.multiple_of(k1 * 128, 128), 128)
        v = jnp.zeros((256, 128), F32)
        for k in range(NT):
            v = v + lax.dot_general(
                cf[k, at, :], pb[k, cols, :], (((1,), (1,)), ((), ())), preferred_element_type=F32
            )
        igrad[at, cols] = v.astype(BF16)
        return 0

    lax.fori_loop(0, 8, part, 0, unroll=2)

    for j in (2, 6):
        f1y_got(yb, zi(j))
        show(yb, zi(j), False)
    for k in range(NY):
        show(k, z, True)
    for j in (2, 6):
        for k in range(NY):
            show(k, zi(j), True)
    for j in (0, 1, 7, 4, 3, 5, 2, 6):
        zz = zi(j)
        f1y_got(yf, zz)
        show(yf, zz, False)
        f1y_got(y2, zz)
        show(y2, zz, False)
        if j in (1, 7, 3, 5, 4):
            f2z_got(zz)
            for k in range(NY):
                show(k, zz, True)
    for d in sent:
        d.wait_send()


def leave(igrad, comb, igrad_out, comb_out, sem):
    copies = [
        pltpu.make_async_copy(
            comb.at[1024 * k : 1024 * (k + 1)], comb_out.at[1024 * k : 1024 * (k + 1)], sem.at[k]
        )
        for k in range(4)
    ]
    copies.append(pltpu.make_async_copy(igrad, igrad_out, sem.at[4]))
    for d in copies:
        d.start()
    for d in copies:
        d.wait()


def on_device(attention, cotangent, projection):
    dma = pltpu.SemaphoreType.DMA

    def hbm(a):
        return pltpu.with_memory_space_constraint(a, pltpu.HBM)

    v = pltpu.VMEM
    igrad, comb = pl.pallas_call(
        body,
        out_shape=(
            jax.ShapeDtypeStruct((512, 512), BF16),
            jax.ShapeDtypeStruct((NY, NZ, 128, 256), F32),
        ),
        in_specs=[pl.BlockSpec(memory_space=pl.ANY)] * 3,
        out_specs=(
            pl.BlockSpec(memory_space=pltpu.VMEM),
            pl.BlockSpec(memory_space=pltpu.VMEM),
        ),
        scratch_shapes=[
            v((H, NT, 16, 512), BF16),
            v((H, NT, NY, 2, 16, 512), BF16),
            v((NY, 512, 256), BF16),
            v((NT, 512, 256), BF16),
            v((NT, 512, 256), BF16),
            v((NY, NZ, 256, 128), F32),
            v((NZ, 256, 128), F32),
            v((NZ, 256, 128), F32),
            v((NZ, 272, 128), BF16),
            v((NZ, 272, 128), BF16),
            v((NY, NZ, 128, 256), BF16),
            v((128, 256), F32),
            v((128, 128), F32),
            v((NY * NT, 8, 128), F32),
            v((NT, 8, 128), F32),
            v((NY * NZ, 8, 128), F32),
            dma((8,)),
            dma((H, NT)),
            dma((H, NT)),
            dma((H, NY)),
            dma((H, NY)),
            dma((H, 7)),
            dma((H, NT)),
            dma((3,)),
            dma((NY,)),
            dma((7,)),
            dma((NT,)),
            dma((NT,)),
            dma((NT,)),
            dma((NY * NT,)),
            dma((NY * NT,)),
            dma((NZ,)),
            dma((NZ,)),
            dma((NT,)),
            dma((NT,)),
            dma((NY * NZ,)),
            dma((NY * NZ,)),
            dma((NZ,)),
            dma((NZ,)),
            dma((3, NZ)),
            dma((NY, NZ)),
            dma((NY,)),
            dma((NY,)),
            dma((7,)),
            dma((NZ,)),
        ],
        compiler_params=pltpu.CompilerParams(
            collective_id=0, has_side_effects=True, vmem_limit_bytes=48 * 1024 * 1024
        ),
        cost_estimate=pl.CostEstimate(
            flops=4 * 2**30, bytes_accessed=16 * 2**20, transcendentals=0
        ),
    )(
        hbm(attention.reshape(H, NT, 16, 512)),
        hbm(cotangent),
        hbm(projection.reshape(NT, 512, 256)),
    )
    return pl.pallas_call(
        leave,
        out_shape=(
            jax.ShapeDtypeStruct((512, 512), BF16),
            jax.ShapeDtypeStruct((4096, 256), F32),
        ),
        in_specs=[pl.BlockSpec(memory_space=pltpu.VMEM)] * 2,
        out_specs=[pl.BlockSpec(memory_space=pltpu.HBM)] * 2,
        scratch_shapes=[dma((5,))],
        compiler_params=pltpu.CompilerParams(vmem_limit_bytes=1024 * 1024),
        cost_estimate=pl.CostEstimate(flops=0, bytes_accessed=9 * 2**20, transcendentals=0),
    )(
        pltpu.with_memory_space_constraint(igrad, pltpu.VMEM),
        pltpu.with_memory_space_constraint(comb.reshape(4096, 256), pltpu.VMEM),
    )


def solution(mesh):
    return jax.shard_map(
        on_device,
        mesh=mesh,
        in_specs=(P("dp", "tensor"), P("dp", "tensor"), P(None, "tensor")),
        out_specs=(P("dp", "tensor"), P(None, "tensor")),
        check_vma=False,
    )
```
